32 devices in a mesh: row: 8 (over z, x), col: 4 (over y, core).
Axes of the slice: x: 2, y: 2, z: 4, core: 2. Of those that a mesh axis runs over, the one named last changes fastest.
Arguments:
- right_side: float32 [6, 8, 64, 128], P(None, 'row'), may hold values from -6 to 6
- inverses: float32 [6, 8, 128, 128], P(None, 'row'), may hold values from -1 to 3
- factor_blocks: bfloat16 [15, 8, 8, 128, 128], P(None, 'row', 'col'), may hold values from -0.15625 to 0.15625
- pattern: int32 [15, 8, 8], P(None, 'row', 'col'), may hold values 0 or 1
Outputs:
- forward_part: float32 [6, 8, 64, 128], P(None, 'row')
- solution: float32 [6, 8, 64, 128], P(None, 'row')
The draws below stay inside these ranges and needn't reach their ends.
All inputs are finite; a program needn't handle non-finite values. No bound on the sum of `pattern` on one device may be relied on, other than what follows from the above.
Results may differ from the reference program's by a relative error of at most 0.014.
Values may be sent and summed in bfloat16 or wider, within the bound.
No kernel may reach another device: no remote copies, remote signals or barrier semaphores. Data moves between devices by JAX's collectives and lax.ppermute only.
A program may use at most 64 MiB of HBM per device.

```python
import math
import jax
import jax.numpy as jnp
from jax import lax

B = 128
NRHS = 64
LEV = 6
W = 8
PAIRS = 15


def draw_inverses(key, part):
    first_key, second_key = jax.random.split(jax.random.fold_in(key, 11))
    diagonal = jnp.exp(jax.random.uniform(first_key, (LEV, W, B), jnp.float32, math.log(0.5), math.log(2.0)))
    noise_part = jax.random.truncated_normal(second_key, -3.0, 3.0, (LEV, W, B, B), jnp.float32) * (0.5 / math.sqrt(B))
    eye_table = jnp.eye(B, dtype=jnp.float32)
    return noise_part + eye_table * diagonal[..., None]


def touch_ends(drawn, own_key, least, high):
    index_at = [jax.random.randint(jax.random.fold_in(own_key, axis), (), 0, length) for axis, length in enumerate(drawn.shape)]
    main_axis = drawn.shape.index(max(drawn.shape))
    neighbour = index_at[:main_axis] + [(index_at[main_axis] + 1) % drawn.shape[main_axis]] + index_at[main_axis + 1:]
    return drawn.at[tuple(index_at)].set(least).at[tuple(neighbour)].set(high)


def spiked(drawn, key, source, target, shards_of, factor):
    owner, partner = [(jnp.arange(drawn.shape[dim]) // (drawn.shape[dim] // shards_of)).reshape([-1 if axis == dim else 1 for axis in range(drawn.ndim)]) for dim in (source, target)]
    chosen = jax.random.permutation(key, shards_of)[partner]
    strong = (owner == chosen) | (owner == (partner + shards_of // 2) % shards_of)
    return jnp.where(strong, factor * drawn, drawn)


def block_levels(key, shape, cuts, least, largest):
    level, own = 1.0, jax.random.fold_in(key, 6)
    for axis_at, shards_of in cuts:
        heights = jnp.exp(jax.random.uniform(jax.random.fold_in(own, axis_at), (shards_of,), jnp.float32, least / len(cuts), largest / len(cuts)))
        level = level * jnp.repeat(heights, shape[axis_at] // shards_of).reshape([-1 if axis == axis_at else 1 for axis in range(len(shape))])
    return level


def gaussian(own_key, dims, deviation, bound, shards=(), held_as=jnp.bfloat16):
    entries = jax.random.normal(own_key, dims, jnp.float32) * deviation
    if len(shards) > 0:
        entries = block_levels(own_key, dims, shards, -0.22, 0.18) * entries
    return jnp.clip(entries, min=-bound, max=bound).astype(held_as)


def heavy_noise(own_key, dims, scale, most, pieces, heavy, held_as=jnp.bfloat16):
    array = scale * jax.random.normal(own_key, dims, jnp.float32)
    if pieces:
        array = array * block_levels(own_key, dims, pieces, -0.22, 0.18)
    return jnp.clip(spiked(array, jax.random.fold_in(own_key, 3), *heavy), -most, most).astype(held_as)


def setup_inputs(seed: int = 0) -> dict:
    keys = jax.random.split(jax.random.key(seed), 5)
    return {
        "right_side": gaussian(keys[0], (LEV, W, NRHS, B), 1.0, 6.0, ((1, 8),), jnp.float32),
        "inverses": draw_inverses(jax.random.fold_in(keys[4], 71), 0),
        "factor_blocks": heavy_noise(keys[2], (PAIRS, W, W, B, B), (B * W * LEV // 2) ** -0.5, 0.15625, ((1, 8), (2, 4)), (1, 2, 8, 2.0)),
        "pattern": touch_ends((jax.random.randint(keys[3], (PAIRS, W, W), 0, 2) < 1).astype(jnp.int32), jax.random.fold_in(keys[3], 1), 0, 1),
    }


def pair_number(higher, lower_level):
    return higher * (higher - 1) // 2 + lower_level


def masked_block(factor_blocks, pattern, pair_index):
    return jnp.where(pattern[pair_index][:, :, None, None] != 0, factor_blocks[pair_index].astype(jnp.float32), jnp.float32(0.0))


def reference(right_side, inverses, factor_blocks, pattern):
    solved = []
    rounded = []
    for height in range(LEV):
        remaining = right_side[height]
        if height > 0:
            update = jnp.zeros(remaining.shape, jnp.float32)
            for earlier in range(height):
                masked = masked_block(factor_blocks, pattern, pair_number(height, earlier))
                update = update + jnp.einsum("ikab,knb->ina", masked, rounded[earlier].astype(jnp.float32))
            remaining = remaining - update
        segment = jnp.einsum("inb,iab->ina", remaining, inverses[height], precision=lax.Precision.HIGHEST)
        solved.append(segment)
        rounded.append(segment.astype(jnp.bfloat16))
    results = [None] * LEV
    settled = [None] * LEV
    for height in range(LEV - 1, -1, -1):
        remaining = solved[height]
        if height < LEV - 1:
            update = jnp.zeros(remaining.shape, jnp.float32)
            for later in range(height + 1, LEV):
                masked = masked_block(factor_blocks, pattern, pair_number(later, height))
                update = update + jnp.einsum("ikab,ina->knb", masked, settled[later].astype(jnp.float32))
            remaining = remaining - update
        segment = jnp.einsum("ina,iab->inb", remaining, inverses[height], precision=lax.Precision.HIGHEST)
        results[height] = segment
        settled[height] = segment.astype(jnp.bfloat16)
    return jnp.stack(solved), jnp.stack(results)
```

```python
import functools
import math
import jax
import jax.numpy as jnp
from jax import lax
from jax.experimental import pallas as pl
from jax.experimental.pallas import tpu as pltpu
from jax.sharding import PartitionSpec as P

HIGHEST = lax.Precision.HIGHEST
VMEM = pl.BlockSpec(memory_space=pltpu.VMEM)
SMEM = pl.BlockSpec(memory_space=pltpu.SMEM)
f32, bf16 = jnp.float32, jnp.bfloat16


def pair_number(higher, lower_level):
    return higher * (higher - 1) // 2 + lower_level


def times_transposed(v, g, precision=None):
    return lax.dot_general(
        v, g, (((1,), (1,)), ((), ())), precision=precision, preferred_element_type=f32
    )


def times(v, g, precision=None):
    return lax.dot_general(
        v, g, (((1,), (0,)), ((), ())), precision=precision, preferred_element_type=f32
    )


def send_all(send_ref, value):
    for k in range(send_ref.shape[0]):
        send_ref[k] = value


def own_rows(col_ref, right_ref, level, chunk):
    return right_ref[level, pl.ds(pl.multiple_of(col_ref[0] * chunk, chunk), chunk), :]


def update(col_ref, terms):
    total = None
    for panels, groups in terms:
        for q, blocks in enumerate(groups):
            width = blocks.shape[0]
            base = (col_ref[0] ^ q) * width
            for j in range(width):
                term = times_transposed(panels[base + j], blocks[j])
                total = term if total is None else total + term
    return total


def downdate(col_ref, parts, terms, out_ref, carried=None):
    for q in range(parts):
        width = terms[0][1][q].shape[0]
        base = (col_ref[0] ^ q) * width
        for j in range(width):
            total = None if carried is None else carried[base + j]
            for value, groups in terms:
                term = times(value, groups[q][j])
                total = term if total is None else total + term
            out_ref[base + j] = total.astype(out_ref.dtype)


def arrived_sum(arrived_ref):
    total = arrived_ref[0].astype(f32)
    for r in range(1, arrived_ref.shape[0]):
        total = total + arrived_ref[r].astype(f32)
    return total


def first_kernel(chunk, col_ref, right_ref, inverse_ref, solved_ref, send_ref):
    value = times_transposed(own_rows(col_ref, right_ref, 0, chunk), inverse_ref[0], HIGHEST)
    solved_ref[...] = value
    send_all(send_ref, value.astype(bf16))


def before_kernel(height, parts, col_ref, right_ref, *refs):
    count = height - 1
    gathered, blocks, out_ref = refs[:count], refs[count:-1], refs[-1]
    value = own_rows(col_ref, right_ref, height, out_ref.shape[0])
    if count:
        terms = [(gathered[l], [b.at[l] for b in blocks]) for l in range(count)]
        value = value - update(col_ref, terms)
    out_ref[...] = value


def forward_kernel(height, parts, col_ref, before_ref, inverse_ref, panels_ref, *refs):
    blocks, (solved_ref, send_ref) = refs[:parts], refs[parts:]
    terms = [(panels_ref, [b.at[height - 1] for b in blocks])]
    value = times_transposed(before_ref[...] - update(col_ref, terms), inverse_ref[height], HIGHEST)
    solved_ref[...] = value
    send_all(send_ref, value.astype(bf16))


def turn_kernel(height, parts, col_ref, before_ref, inverse_ref, panels_ref, *refs):
    blocks, (solved_ref, result_ref, settled_ref, send_ref) = refs[:parts], refs[parts:]
    groups = [b.at[height - 1] for b in blocks]
    value = times_transposed(
        before_ref[...] - update(col_ref, [(panels_ref, groups)]), inverse_ref[height], HIGHEST
    )
    solved_ref[...] = value
    result = times(value, inverse_ref[height], HIGHEST)
    result_ref[...] = result
    settled = result.astype(bf16)
    settled_ref[...] = settled
    downdate(col_ref, parts, [(settled, groups)], send_ref)


def after_kernel(height, parts, col_ref, *refs):
    count = len(refs[:-1]) // (parts + 1)
    settled, blocks, out_ref = refs[:count], refs[count:-1], refs[-1]
    terms = [
        (settled[s][...], [b.at[height] for b in blocks[s * parts : (s + 1) * parts]])
        for s in range(count)
    ]
    downdate(col_ref, parts, terms, out_ref)


def backward_kernel(height, parts, carries, col_ref, solved_ref, inverse_ref, arrived_ref, *refs):
    blocks, (result_ref, settled_ref, send_ref) = refs[carries : carries + parts], refs[-3:]
    result = times(solved_ref[...] - arrived_sum(arrived_ref), inverse_ref[height], HIGHEST)
    result_ref[...] = result
    settled = result.astype(bf16)
    settled_ref[...] = settled
    groups = [b.at[height - 1] for b in blocks]
    downdate(col_ref, parts, [(settled, groups)], send_ref, refs[0] if carries else None)


def last_kernel(solved_ref, inverse_ref, arrived_ref, result_ref):
    result_ref[0] = times(solved_ref[...] - arrived_sum(arrived_ref), inverse_ref[0], HIGHEST)


def join_kernel(parts, low_parts, col_ref, *refs):
    runs, out_ref = refs[:-1], refs[-1]
    at = 0
    for start in range(0, len(runs), parts):
        depth, chunk = runs[start].shape[:2]
        for q in range(parts):
            rows = pl.ds(pl.multiple_of((col_ref[0] ^ q) * chunk, chunk), chunk)
            out_ref[pl.ds(at, depth), rows, :] = runs[start + q][...]
        at += depth


def stack_kernel(*refs):
    for s, ref in enumerate(refs[:-1]):
        refs[-1][s] = ref[...]


def call(kernel, name, shapes, *operands):
    held = sum(math.prod(s) * jnp.dtype(d).itemsize for s, d in shapes)
    held += sum(o.size * o.dtype.itemsize for o in operands)
    return pl.pallas_call(
        kernel,
        name=name,
        out_shape=[jax.ShapeDtypeStruct(s, d) for s, d in shapes],
        in_specs=[SMEM if o.shape == (1,) else VMEM for o in operands],
        out_specs=[VMEM] * len(shapes),
        compiler_params=pltpu.CompilerParams(vmem_limit_bytes=held + (2 << 20)),
    )(*operands)


def exchange(value, step, size):
    return lax.ppermute(value, "col", [(c, c ^ step) for c in range(size)])


def shards(rows, cols, right_side, inverses, factor_blocks, pattern):
    levels, _, rhs, depth = right_side.shape
    chunk = rhs // cols
    col = lax.axis_index("col").reshape(1).astype(jnp.int32)
    right, inverse = right_side[:, 0], inverses[:, 0]
    panel, sent = (chunk, depth), (rows, chunk, depth)
    steps = [1 << s for s in reversed(range((cols - 1).bit_length()))]

    def swap(value):
        return lax.all_to_all(value, "row", 0, 0)

    def level_blocks(level):
        low, high = pair_number(level, 0), pair_number(level + 1, 0)
        held = {
            0: jnp.where(
                pattern[low:high, 0, :, None, None] != 0,
                factor_blocks[low:high, 0],
                jnp.zeros((), factor_blocks.dtype),
            )
        }
        for step in steps:
            for q, value in list(held.items()):
                held[q ^ step] = exchange(value, step, cols)
        return [held[q] for q in range(cols)]

    value, send = call(
        functools.partial(first_kernel, chunk), "forward_0", [(panel, f32), (sent, bf16)], col, right, inverse
    )
    solved, gathered = [value], [swap(send)]
    blocks = [None] + [level_blocks(level) for level in range(1, levels)]
    top = levels - 1
    results, settled = [None] * levels, [None] * levels
    for height in range(1, levels):
        lower = blocks[height] if height > 1 else []
        before, = call(
            functools.partial(before_kernel, height, cols), f"before_{height}", [(panel, f32)],
            col, right, *gathered[: height - 1], *lower,
        )
        operands = (col, before, inverse, gathered[height - 1], *blocks[height])
        if height < top:
            value, send = call(
                functools.partial(forward_kernel, height, cols), f"forward_{height}",
                [(panel, f32), (sent, bf16)], *operands,
            )
            gathered.append(swap(send))
        else:
            value, results[top], settled[top], send = call(
                functools.partial(turn_kernel, height, cols), "turn",
                [(panel, f32), (panel, f32), (panel, bf16), (sent, bf16)], *operands,
            )
        solved.append(value)
    for height in range(top - 1, 0, -1):
        arrived = swap(send)
        carried = []
        if height + 1 <= top:
            upper = range(height + 1, levels)
            carried = call(
                functools.partial(after_kernel, height - 1, cols), f"after_{height - 1}", [(sent, f32)],
                col, *[settled[l] for l in upper], *[b for l in upper for b in blocks[l]],
            )
        results[height], settled[height], send = call(
            functools.partial(backward_kernel, height, cols, len(carried)), f"backward_{height}",
            [(panel, f32), (panel, bf16), (sent, bf16)],
            col, solved[height], inverse, arrived, *carried, *blocks[height],
        )
    arrived = swap(send)
    result, = call(last_kernel, "backward_0", [((1,) + panel, f32)], solved[0], inverse, arrived)

    def pieces(value):
        return [value] + [exchange(value, q, cols) for q in range(1, cols)]

    def stacked(panels, name):
        return call(stack_kernel, name, [((len(panels),) + panel, f32)], *panels)[0]

    def joined(name, *runs):
        return call(
            functools.partial(join_kernel, cols, 0), name, [((levels, rhs, depth), f32)],
            col, *[p for run in runs for p in run],
        )[0][:, None]

    upper = pieces(stacked(results[1:], "stack_results"))
    forward = joined("join_solved", pieces(stacked(solved, "stack_solved")))
    return forward, joined("join_results", pieces(result), upper)


def solution(mesh):
    rows, cols = mesh.shape["row"], mesh.shape["col"]
    placed = (
        P(None, "row", None, None),
        P(None, "row", None, None),
        P(None, "row", "col", None, None),
        P(None, "row", "col"),
    )
    return jax.shard_map(
        functools.partial(shards, rows, cols),
        mesh=mesh,
        in_specs=placed,
        out_specs=(P(None, "row", None, None), P(None, "row", None, None)),
        check_vma=False,
    )
```

```python
import functools
import math
import jax
import jax.numpy as jnp
from jax import lax
from jax.experimental import pallas as pl
from jax.experimental.pallas import tpu as pltpu
from jax.sharding import PartitionSpec as P

FINE = lax.Precision.HIGHEST
MERGE_BYTES = 24 << 20
f32, bf16 = jnp.float32, jnp.bfloat16


def pair_number(higher, lower_level):
    return higher * (higher - 1) // 2 + lower_level


def times_transposed(v, g, precision=None):
    return lax.dot_general(
        v, g, (((1,), (1,)), ((), ())), precision=precision, preferred_element_type=f32
    )


def times(v, g, precision=None):
    return lax.dot_general(
        v, g, (((1,), (0,)), ((), ())), precision=precision, preferred_element_type=f32
    )


def split_product(d, g):
    high = d.astype(bf16)
    low = (d - high.astype(f32)).astype(bf16)
    return times(high, g) + times(low, g)


def kernel_call(body, ins, outs):
    in_keys, out_keys = list(ins), list(outs)
    arrays, specs, held = [], [], 0
    for value in ins.values():
        array, at = value if isinstance(value, tuple) else (value, -1)
        if array.dtype == jnp.int32:
            specs.append(pl.BlockSpec(memory_space=pltpu.SMEM))
        elif at is None:
            specs.append(pl.BlockSpec(memory_space=pl.ANY))
        else:
            shape = array.shape
            if at >= 0:
                shape = (1,) + shape[1:]
                array = pltpu.with_memory_space_constraint(array, pltpu.HBM)
            index = (max(at, 0),) + (0,) * (len(shape) - 1)
            specs.append(pl.BlockSpec(shape, lambda *_, index=index: index))
            held += math.prod(shape) * array.dtype.itemsize
        arrays.append(array)
    shapes = list(outs.values())
    if len(shapes) == 1:
        shapes.append(((8, 128), f32))
    held += sum(math.prod(s) * jnp.dtype(d).itemsize for s, d in shapes)

    def kernel(*refs):
        body(dict(zip(in_keys + out_keys, refs)))
        if len(out_keys) == 1:
            refs[-1][...] = jnp.zeros(refs[-1].shape, f32)

    values = pl.pallas_call(
        kernel,
        grid=(1,),
        out_shape=[pltpu.HBM(s, d) for s, d in shapes],
        in_specs=specs,
        out_specs=[pl.BlockSpec(s, lambda *_, d=len(s): (0,) * d) for s, d in shapes],
        compiler_params=pltpu.CompilerParams(vmem_limit_bytes=2 * held + (3 << 20)),
    )(*arrays)
    return dict(zip(out_keys, values))


def exchange(value, step, size):
    return lax.ppermute(value, "col", [(c, c ^ step) for c in range(size)])


def shards(rows, cols, right_side, inverses, factor_blocks, pattern):
    return body_of(rows, cols, right_side, inverses, factor_blocks, pattern)


def body_of(rows, cols, right_side, inverses, factor_blocks, pattern):
    levels, _, rhs, depth = right_side.shape
    width = factor_blocks.shape[2]
    chunk = rhs // cols
    top = levels - 1
    col = lax.axis_index("col").reshape(1).astype(jnp.int32)
    row = lax.axis_index("row").reshape(1).astype(jnp.int32)
    panel, sent = (chunk, depth), (rows, chunk, depth)
    block = depth * depth * factor_blocks.dtype.itemsize
    sizes = factor_blocks.shape[0] * cols * width * block + 6 * rows * width * block
    merging = sizes <= MERGE_BYTES and levels % 2 == 0 and rows & (rows - 1) == 0
    merged = range(0, top - 1, 2) if merging else ()
    steps = [1 << s for s in reversed(range((cols - 1).bit_length()))]

    COL, ROW, PATTERN, BLOCKS, WAIT, PRE, ARRIVED, CARRY, SEND, OUT, ALL = range(11)
    INV, RIGHT, PANEL, X, Y, V, RAW, FAR = range(11, 19)

    def inv(*ms):
        return {(INV, m): (inverses, m) for m in ms}

    def right(m):
        return {(RIGHT, m): (right_side, m)}

    def own(r, m):
        return r[RIGHT, m][0, 0, pl.ds(pl.multiple_of(r[COL][0] * chunk, chunk), chunk), :]

    def swap(value):
        return lax.all_to_all(value, "row", 0, 0)

    def send_all(r, value):
        for k in range(rows):
            r[SEND][k] = value

    cuts = [(1, 2), (2, 4), (4, levels)]
    bundles = {n: [(m, l) for m in range(*cut) for l in range(m)] for n, cut in zip("abc", cuts)}
    place = {pair: (n, s) for n, pairs in bundles.items() for s, pair in enumerate(pairs)}
    held, arrays = {}, {}

    def shape_of(pairs):
        return (len(pairs), width, depth, depth), bf16

    def add_bundle(name):
        found = {0: held[name]}
        for step in steps:
            found |= {q ^ step: exchange(v, step, cols) for q, v in found.items()}
        for q, v in found.items():
            arrays[name, q] = v

    def need(*keys):
        found = {}
        for n, s in sorted({place[k] for k in keys}):
            for q in range(cols):
                v = arrays[n, q]
                found[n, s, q] = v if v.shape[0] == 1 else (v, s)
        return found

    def groups(r, key):
        name, s = place[key]
        return [r[name, s, q].at[0] for q in range(cols)]

    def column(r, q, j):
        return (r[COL][0] ^ q) * width + j

    def sum_over(r, m, lower):
        total = None
        for l in lower:
            for q, blocks in enumerate(groups(r, (m, l))):
                for j in range(width):
                    term = times_transposed(r[PANEL, l][column(r, q, j)], blocks[j])
                    total = term if total is None else total + term
        return total

    def spread_sums(r, terms, out_ref, slot, carried=None):
        for q in range(cols):
            for j in range(width):
                k = column(r, q, j)
                total = None if carried is None else carried[k, slot]
                for value, key in terms:
                    term = times(value, groups(r, key)[q][j])
                    total = term if total is None else total + term
                out_ref[k, slot] = total.astype(out_ref.dtype)

    def masked(r, p, at, j):
        value = r[BLOCKS][at, 0, j]
        return jnp.where(r[PATTERN][p, 0, j] != 0, value, jnp.zeros_like(value))

    def first_body(r):
        value = times_transposed(own(r, 0), r[INV, 0][0, 0], FINE)
        r[X][...] = value
        send_all(r, value.astype(bf16))
        for j in range(width):
            r[OUT][0, j] = masked(r, 0, 0, j)

    out = kernel_call(
        first_body,
        {COL: col, PATTERN: pattern, BLOCKS: (factor_blocks, 0), **right(0), **inv(0)},
        {X: (panel, f32), SEND: (sent, bf16), OUT: shape_of("a")},
    )
    x = {0: out[X]}
    held["a"] = out[OUT]

    def mask_body(r):
        for name, pairs in bundles.items():
            for s, (m, l) in enumerate(pairs):
                for j in range(width):
                    value = masked(r, pair_number(m, l), pair_number(m, l), j)
                    if name in r:
                        r[name][s, j] = value
                    if l in merged and m == l + 1:
                        product = split_product(r[INV, m][0, 0], value)
                        r[OUT][l // 2, :, j * depth : (j + 1) * depth] = product.astype(bf16)

    outs = {n: shape_of(pairs) for n, pairs in bundles.items() if n != "a"}
    if merged:
        outs[OUT] = ((len(merged), depth, width * depth), bf16)
    found = kernel_call(
        mask_body,
        {PATTERN: pattern, BLOCKS: factor_blocks, WAIT: (out[SEND], None), **inv(*[l + 1 for l in merged])}, outs,
    )
    product = found.pop(OUT, None)
    held |= found
    for name in bundles:
        add_bundle(name)

    products = {0: product}
    if merged:
        for d in [1 << s for s in reversed(range((rows - 1).bit_length()))]:
            products |= {s ^ d: lax.ppermute(v, "row", [(r, r ^ d) for r in range(rows)]) for s, v in products.items()}

    gathered = {0: swap(out[SEND])}
    y, rounded = {}, {}

    def panels(lower):
        return {(PANEL, l): gathered[l] for l in lower}

    for m in range(1, levels):
        def pre_body(r):
            r[PRE][...] = own(r, m) - sum_over(r, m, range(m - 1))

        pre = right(m)
        if m > 1:
            pre = kernel_call(
                pre_body,
                {COL: col, **pre, **panels(range(m - 1)), **need(*[(m, l) for l in range(m - 1)])},
                {PRE: (panel, f32)},
            )

        def solve_body(r):
            rest = r[PRE][...] if PRE in r else own(r, m)
            value = times_transposed(rest - sum_over(r, m, [m - 1]), r[INV, m][0, 0], FINE)
            r[X][...] = value
            if m < top:
                send_all(r, value.astype(bf16))
                return
            result = times(value, r[INV, m][0, 0], FINE)
            r[Y][...] = result
            r[V][...] = result.astype(bf16)
            spread_sums(r, [(result.astype(bf16), (m, m - 1))], r[SEND], 0)

        outs = {X: (panel, f32), SEND: (sent, bf16)}
        if m == top:
            outs = {X: (panel, f32), Y: (panel, f32), V: (panel, bf16), SEND: ((rows, 1, chunk, depth), bf16)}
        out = kernel_call(solve_body, {COL: col, **pre, **inv(m), **panels([m - 1]), **need((m, m - 1))}, outs)
        x[m] = out[X]
        if m < top:
            gathered[m] = swap(out[SEND])
    y[top], rounded[top] = out[Y], out[V]

    wanted = [(m, l) for l in merged for m in range(l + 2, levels)]
    if merged:
        def fix_body(r):
            for s in range(rows):
                r[ALL][r[ROW][0] ^ s] = r[FAR, s][...]
            for s, (m, l) in enumerate(wanted):
                total = None
                for q, blocks in enumerate(groups(r, (m, l + 1))):
                    for j in range(width):
                        term = times(blocks[j], r[ALL][column(r, q, j), l // 2])
                        total = term if total is None else total + term
                for j in range(width):
                    raw = r[RAW, m, l][0, j].astype(f32)
                    r[OUT][s, j] = (raw - total[:, j * depth : (j + 1) * depth]).astype(bf16)

        raws = {(RAW, m, l): (held[place[m, l][0]], place[m, l][1]) for m, l in wanted}
        held["d"] = kernel_call(
            fix_body,
            {COL: col, ROW: row, **{(FAR, s): v for s, v in products.items()}, **raws}
            | need(*[(m, l + 1) for m, l in wanted]),
            {OUT: shape_of(wanted), ALL: ((rows,) + product.shape, bf16)},
        )[OUT]
        add_bundle("d")
        for s, (m, l) in enumerate(wanted):
            place[m, l, True] = ("d", s)

    lower = [(l, l + 1) for l in reversed(merged)] if merged else [(l,) for l in range(top - 2, -1, -1)]
    plan = [(top - 1,)] + lower

    def terms_for(l, values):
        return [(v, (m, l, True) if (m, l) in wanted else (m, l)) for m, v in values.items()]

    def pairs_for(targets, upper):
        return need(*[key for l in targets for _, key in terms_for(l, dict.fromkeys(upper))])

    for s, done in enumerate(plan):
        targets = plan[s + 1] if s + 1 < len(plan) else ()
        upper = range(done[-1] + 1, levels)
        arrived = swap(out[SEND])
        slots = (rows, max(len(targets), 1), chunk, depth)
        ins = {COL: col, ARRIVED: arrived, **inv(*done), **{(X, m): x[m] for m in done}}
        if targets:
            odds = [l + 1 for l in targets if l in merged]

            def carry_body(r):
                values = {m: r[V, m][...] for m in upper}
                for slot, l in enumerate(targets):
                    terms = terms_for(l, values)
                    if l + 1 in odds:
                        own_part = times(r[X, l + 1][...], r[INV, l + 1][0, 0], FINE).astype(bf16)
                        terms.append((own_part, (l + 1, l)))
                    spread_sums(r, terms, r[CARRY], slot)

            carry = kernel_call(
                carry_body,
                {COL: col, **{(V, m): rounded[m] for m in upper}, **{(X, m): x[m] for m in odds}, **inv(*odds)}
                | pairs_for(targets, upper) | need(*[(m, m - 1) for m in odds]),
                {CARRY: (slots, f32)},
            )
            ins |= {**carry, **pairs_for(targets, done)}

        def step_body(r):
            values = {}
            for slot, m in enumerate(done):
                total = r[ARRIVED][0, slot].astype(f32)
                for k in range(1, rows):
                    total = total + r[ARRIVED][k, slot].astype(f32)
                result = times(r[X, m][...] - total, r[INV, m][0, 0], FINE)
                if not targets:
                    r[OUT][slot] = result
                    continue
                r[Y, m][...] = result
                values[m] = result.astype(bf16)
                r[V, m][...] = values[m]
            for slot, l in enumerate(targets):
                spread_sums(r, terms_for(l, values), r[SEND], slot, r[CARRY])

        if targets:
            outs = {(Y, m): (panel, f32) for m in done} | {(V, m): (panel, bf16) for m in done} | {SEND: (slots, bf16)}
        else:
            outs = {OUT: ((len(done),) + panel, f32)}
        out = kernel_call(step_body, ins, outs)
        if targets:
            for m in done:
                y[m], rounded[m] = out[Y, m], out[V, m]

    def pieces(value):
        return [value] + [exchange(value, q, cols) for q in range(1, cols)]

    def stacked(values):
        def stack_body(r):
            for s in range(len(values)):
                r[OUT][s] = r[X, s][...]

        return kernel_call(
            stack_body, {(X, s): v for s, v in enumerate(values)}, {OUT: ((len(values),) + panel, f32)}
        )[OUT]

    def joined(*runs):
        def join_body(r):
            at = 0
            for s, run in enumerate(runs):
                count = run[0].shape[0]
                for q in range(cols):
                    where = pl.ds(pl.multiple_of((r[COL][0] ^ q) * chunk, chunk), chunk)
                    r[OUT][pl.ds(at, count), where, :] = r[X, s, q][...]
                at += count

        ins = {(X, s, q): v for s, run in enumerate(runs) for q, v in enumerate(run)}
        return kernel_call(join_body, {COL: col, **ins}, {OUT: ((levels, rhs, depth), f32)})[OUT][:, None]

    high = pieces(stacked([y[m] for m in range(len(plan[-1]), levels)]))
    forward = joined(pieces(stacked([x[m] for m in range(levels)])))
    return forward, joined(pieces(out[OUT]), high)


def solution(mesh):
    rows, cols = mesh.shape["row"], mesh.shape["col"]
    placed = (
        P(None, "row", None, None),
        P(None, "row", None, None),
        P(None, "row", "col", None, None),
        P(None, "row", "col"),
    )
    return jax.shard_map(
        functools.partial(shards, rows, cols),
        mesh=mesh,
        in_specs=placed,
        out_specs=(P(None, "row", None, None), P(None, "row", None, None)),
        check_vma=False,
    )
```

```python
import functools
import math
import jax
import jax.numpy as jnp
from jax import lax
from jax.experimental import pallas as pl
from jax.experimental.pallas import tpu as pltpu
from jax.sharding import PartitionSpec as P

FINE = lax.Precision.HIGHEST
MERGE_BYTES = 24 << 20
f32, bf16 = jnp.float32, jnp.bfloat16
ANYWHERE = -2


def pair_number(higher, lower_level):
    return higher * (higher - 1) // 2 + lower_level


def times_transposed(v, g, precision=None):
    return lax.dot_general(
        v, g, (((1,), (1,)), ((), ())), precision=precision, preferred_element_type=f32
    )


def times(v, g, precision=None):
    return lax.dot_general(
        v, g, (((1,), (0,)), ((), ())), precision=precision, preferred_element_type=f32
    )


def split_product(d, g):
    high = d.astype(bf16)
    low = (d - high.astype(f32)).astype(bf16)
    return times(high, g) + times(low, g)


def kernel_call(body, ins, outs, scratch=None):
    in_keys, out_keys, scratch = list(ins), list(outs), scratch or {}
    arrays, specs, held = [], [], 0
    for value in ins.values():
        array, at = value if isinstance(value, tuple) else (value, -1)
        if array.dtype == jnp.int32:
            specs.append(pl.BlockSpec(memory_space=pltpu.SMEM))
        elif at is None:
            specs.append(pl.BlockSpec(memory_space=pl.ANY))
        else:
            shape = array.shape
            if at >= 0:
                shape = (1,) + shape[1:]
            if at > -2:
                array = pltpu.with_memory_space_constraint(array, pltpu.HBM)
            index = (max(at, 0),) + (0,) * (len(shape) - 1)
            specs.append(pl.BlockSpec(shape, lambda *_, index=index: index))
            held += math.prod(shape) * array.dtype.itemsize
        arrays.append(array)
    shapes = list(outs.values())
    if len(shapes) == 1:
        shapes.append(((8, 128), f32))
    held += sum(math.prod(s[0]) * jnp.dtype(s[1]).itemsize for s in shapes)

    def kernel(*refs):
        spare = [None] * (len(shapes) - len(out_keys))
        body(dict(zip(in_keys + out_keys + spare + list(scratch), refs)))
        if spare:
            last = refs[len(in_keys) + 1]
            last[...] = jnp.zeros(last.shape, f32)

    values = pl.pallas_call(
        kernel,
        grid=(1,),
        out_shape=[(pltpu.VMEM if len(s) > 2 else pltpu.HBM)(s[0], s[1]) for s in shapes],
        in_specs=specs,
        out_specs=[pl.BlockSpec(s[0], lambda *_, d=len(s[0]): (0,) * d) for s in shapes],
        scratch_shapes=[pltpu.VMEM(*s) for s in scratch.values()],
        compiler_params=pltpu.CompilerParams(vmem_limit_bytes=2 * held + (4 << 20)),
    )(*arrays)
    return dict(zip(out_keys, values))


def exchange(value, step, size):
    return lax.ppermute(value, "col", [(c, c ^ step) for c in range(size)])


def shards(rows, cols, right_side, inverses, factor_blocks, pattern):
    return body_of(rows, cols, right_side, inverses, factor_blocks, pattern)


def body_of(rows, cols, right_side, inverses, factor_blocks, pattern):
    levels, _, rhs, depth = right_side.shape
    width = factor_blocks.shape[2]
    chunk = rhs // cols
    top = levels - 1
    col = lax.axis_index("col").reshape(1).astype(jnp.int32)
    row = lax.axis_index("row").reshape(1).astype(jnp.int32)
    panel, sent = (chunk, depth), (rows, chunk, depth)
    block = depth * depth * factor_blocks.dtype.itemsize
    sizes = factor_blocks.shape[0] * cols * width * block + 6 * rows * width * block
    merging = sizes <= MERGE_BYTES and levels % 2 == 0 and rows & (rows - 1) == 0
    merged = range(0, top - 1, 2) if merging else ()
    steps = [1 << s for s in reversed(range((cols - 1).bit_length()))]

    COL, ROW, PATTERN, BLOCKS, WAIT, ARRIVED, CARRY, SEND, OUT, ALL = range(10)
    INV, RIGHT, PANEL, X, Y, V, _, FAR = range(10, 18)

    def inv(*ms):
        return {(INV, m): (inverses, m) for m in ms}

    def right(m):
        return {(RIGHT, m): (right_side, m)}

    def own(r, m):
        return r[RIGHT, m][0, 0, pl.ds(pl.multiple_of(r[COL][0] * chunk, chunk), chunk), :]

    def swap(value):
        return lax.all_to_all(value, "row", 0, 0)

    def send_all(r, value):
        for k in range(rows):
            r[SEND][k] = value

    cuts = [(1, 2), (2, 4), (4, levels)]
    bundles = {n: [(m, l) for m in range(*cut) for l in range(m)] for n, cut in zip("abc", cuts)}
    place = {pair: (n, s) for n, pairs in bundles.items() for s, pair in enumerate(pairs)}
    held, arrays = {}, {}

    def near(name, q):
        return merging and q > 0 and name in "bc"

    def shape_of(pairs):
        return (len(pairs), width, depth, depth), bf16

    def add_bundle(name):
        found = {0: held[name]}
        for step in steps:
            found |= {q ^ step: exchange(v, step, cols) for q, v in found.items()}
        for q, v in found.items():
            arrays[name, q] = pltpu.with_memory_space_constraint(v, pltpu.VMEM) if near(name, q) else v

    def need(*keys):
        found = {}
        for n, s in sorted({place[k] for k in keys}):
            for q in range(cols):
                v = arrays[n, q]
                if near(n, q):
                    found[n, q] = (v, ANYWHERE)
                else:
                    found[n, s, q] = (v, ANYWHERE if v.shape[0] == 1 else s)
        return found

    def groups(r, key):
        name, s = place[key]
        return [r[name, q].at[s] if near(name, q) else r[name, s, q].at[0] for q in range(cols)]

    def column(r, q, j):
        return (r[COL][0] ^ q) * width + j

    def sum_over(r, m, lower):
        total = None
        for l in lower:
            for q, blocks in enumerate(groups(r, (m, l))):
                for j in range(width):
                    term = times_transposed(r[PANEL, l][column(r, q, j)], blocks[j])
                    total = term if total is None else total + term
        return total

    def spread_sums(r, terms, out_ref, slot, carried=None):
        for q in range(cols):
            for j in range(width):
                k = column(r, q, j)
                total = None if carried is None else carried[k, slot]
                for value, key in terms:
                    term = times(value, groups(r, key)[q][j])
                    total = term if total is None else total + term
                out_ref[k, slot] = total.astype(out_ref.dtype)

    def masked(r, p, at, j):
        value = r[BLOCKS][at, 0, j]
        return jnp.where(r[PATTERN][p, 0, j] != 0, value, jnp.zeros_like(value))

    def first_body(r):
        value = times_transposed(own(r, 0), r[INV, 0][0, 0], FINE)
        r[X][...] = value
        send_all(r, value.astype(bf16))
        for j in range(width):
            r[OUT][0, j] = masked(r, 0, 0, j)

    out = kernel_call(
        first_body,
        {COL: col, PATTERN: pattern, BLOCKS: (factor_blocks, 0), **right(0), **inv(0)},
        {X: (panel, f32), SEND: (sent, bf16), OUT: shape_of("a")},
    )
    x = {0: out[X]}
    held["a"] = out[OUT]

    def mask_body(r):
        for name, pairs in bundles.items():
            for s, (m, l) in enumerate(pairs):
                for j in range(width):
                    value = masked(r, pair_number(m, l), pair_number(m, l), j)
                    if name in r:
                        r[name][s, j] = value
                    if l in merged and m == l + 1:
                        product = split_product(r[INV, m][0, 0], value)
                        r[OUT][l // 2, :, j * depth : (j + 1) * depth] = product.astype(bf16)

    outs = {n: shape_of(pairs) for n, pairs in bundles.items() if n != "a"}
    if merged:
        outs[OUT] = ((len(merged), depth, width * depth), bf16)
    found = kernel_call(
        mask_body,
        {PATTERN: pattern, BLOCKS: factor_blocks, WAIT: (out[SEND], None), **inv(*[l + 1 for l in merged])}, outs,
    )
    product = found.pop(OUT, None)
    held |= found
    for name in bundles:
        add_bundle(name)

    products = {0: product}
    if merged:
        for d in [1 << s for s in reversed(range((rows - 1).bit_length()))]:
            products |= {s ^ d: lax.ppermute(v, "row", [(r, r ^ d) for r in range(rows)]) for s, v in products.items()}

    gathered = {0: (swap(out[SEND]), ANYWHERE)}
    y, rounded = {}, {}

    def panels(lower):
        return {(PANEL, l): gathered[l] for l in lower}

    for m in range(1, levels):
        def solve_body(r):
            value = times_transposed(own(r, m) - sum_over(r, m, range(m)), r[INV, m][0, 0], FINE)
            r[X][...] = value
            if m < top:
                send_all(r, value.astype(bf16))
                return
            result = times(value, r[INV, m][0, 0], FINE)
            r[Y][...] = result
            r[V][...] = result.astype(bf16)
            spread_sums(r, [(result.astype(bf16), (m, m - 1))], r[SEND], 0)

        outs = {X: (panel, f32), SEND: (sent, bf16)}
        if m == top:
            outs = {X: (panel, f32), Y: (panel, f32), V: (panel, bf16), SEND: ((rows, 1, chunk, depth), bf16)}
        out = kernel_call(
            solve_body,
            {COL: col, **right(m), **inv(m), **panels(range(m)), **need(*[(m, l) for l in range(m)])}, outs,
        )
        x[m] = out[X]
        if m < top:
            gathered[m] = (swap(out[SEND]), ANYWHERE)
    y[top], rounded[top] = out[Y], out[V]

    wanted = [(m, l) for l in merged for m in range(l + 2, levels)]
    if merged:
        def fix_body(r):
            for s in range(rows):
                r[ALL][r[ROW][0] ^ s] = r[FAR, s][...]
            for s, (m, l) in enumerate(wanted):
                total = None
                for q, blocks in enumerate(groups(r, (m, l + 1))):
                    for j in range(width):
                        term = times(blocks[j], r[ALL][column(r, q, j), l // 2])
                        total = term if total is None else total + term
                for j in range(width):
                    raw = groups(r, (m, l))[0][j].astype(f32)
                    r[OUT][s, j] = (raw - total[:, j * depth : (j + 1) * depth]).astype(bf16)

        held["d"] = kernel_call(
            fix_body,
            {COL: col, ROW: row, **{(FAR, s): (v, ANYWHERE) for s, v in products.items()}}
            | need(*wanted, *[(m, l + 1) for m, l in wanted]),
            {OUT: shape_of(wanted)}, {ALL: ((rows,) + product.shape, bf16)},
        )[OUT]
        add_bundle("d")
        for s, (m, l) in enumerate(wanted):
            place[m, l, True] = ("d", s)

    lower = [(l, l + 1) for l in reversed(merged)] if merged else [(l,) for l in range(top - 2, -1, -1)]
    plan = [(top - 1,)] + lower

    def terms_for(l, values):
        return [(v, (m, l, True) if (m, l) in wanted else (m, l)) for m, v in values.items()]

    def pairs_for(targets, upper):
        return need(*[key for l in targets for _, key in terms_for(l, dict.fromkeys(upper))])

    for s, done in enumerate(plan):
        targets = plan[s + 1] if s + 1 < len(plan) else ()
        upper = range(done[-1] + 1, levels)
        arrived = (swap(out[SEND]), ANYWHERE)
        slots = (rows, max(len(targets), 1), chunk, depth)
        ins = {COL: col, ARRIVED: arrived, **inv(*done), **{(X, m): x[m] for m in done}}
        if targets:
            odds = [l + 1 for l in targets if l in merged]

            def carry_terms(r):
                values = {m: r[V, m][...] for m in upper}
                terms = {l: terms_for(l, values) for l in targets}
                for m in odds:
                    own_part = times(r[X, m][...], r[INV, m][0, 0], FINE).astype(bf16)
                    terms[m - 1].append((own_part, (m, m - 1)))
                return terms

            known = {(V, m): rounded[m] for m in upper} | {(X, m): x[m] for m in odds} | inv(*odds)
            known |= pairs_for(targets, upper) | need(*[(m, m - 1) for m in odds])
            if s > 0:
                def carry_body(r):
                    for slot, (l, terms) in enumerate(carry_terms(r).items()):
                        spread_sums(r, terms, r[CARRY], slot)

                known = kernel_call(carry_body, {COL: col, **known}, {CARRY: (slots, f32)})
            ins |= {**known, **pairs_for(targets, done)}

        def step_body(r):
            values = {}
            for slot, m in enumerate(done):
                total = r[ARRIVED][0, slot].astype(f32)
                for k in range(1, rows):
                    total = total + r[ARRIVED][k, slot].astype(f32)
                result = times(r[X, m][...] - total, r[INV, m][0, 0], FINE)
                if not targets:
                    r[OUT][slot] = result
                    continue
                r[Y, m][...] = result
                values[m] = result.astype(bf16)
                r[V, m][...] = values[m]
            folded = carry_terms(r) if targets and s == 0 else {}
            for slot, l in enumerate(targets):
                spread_sums(r, terms_for(l, values) + folded.get(l, []), r[SEND], slot, r.get(CARRY))

        if targets:
            outs = {(Y, m): (panel, f32) for m in done} | {(V, m): (panel, bf16) for m in done} | {SEND: (slots, bf16)}
        else:
            outs = {OUT: ((len(done),) + panel, f32)}
        out = kernel_call(step_body, ins, outs)
        if targets:
            for m in done:
                y[m], rounded[m] = out[Y, m], out[V, m]

    def pieces(value):
        found = {q: exchange(value, q, cols) for q in range(cols - 1, 0, -1)}
        return [value] + [found[q] for q in range(1, cols)]

    def stacked(values):
        def stack_body(r):
            for s in range(len(values)):
                r[OUT][s] = r[X, s][...]

        return kernel_call(
            stack_body, {(X, s): v for s, v in enumerate(values)}, {OUT: ((len(values),) + panel, f32)}
        )[OUT]

    def joined(*runs):
        def join_body(r):
            at = 0
            for s, run in enumerate(runs):
                count = run[0].shape[0]
                for q in range(cols):
                    where = pl.ds(pl.multiple_of((r[COL][0] ^ q) * chunk, chunk), chunk)
                    r[OUT][pl.ds(at, count), where, :] = r[X, s, q][...]
                at += count

        ins = {(X, s, q): (v, ANYWHERE if q else -1) for s, run in enumerate(runs) for q, v in enumerate(run)}
        return kernel_call(join_body, {COL: col, **ins}, {OUT: ((levels, rhs, depth), f32)})[OUT][:, None]

    high = pieces(stacked([y[m] for m in range(len(plan[-1]), levels)]))
    forward = joined(pieces(stacked([x[m] for m in range(levels)])))
    return forward, joined(pieces(out[OUT]), high)


def solution(mesh):
    rows, cols = mesh.shape["row"], mesh.shape["col"]
    placed = (
        P(None, "row", None, None),
        P(None, "row", None, None),
        P(None, "row", "col", None, None),
        P(None, "row", "col"),
    )
    return jax.shard_map(
        functools.partial(shards, rows, cols),
        mesh=mesh,
        in_specs=placed,
        out_specs=(P(None, "row", None, None), P(None, "row", None, None)),
        check_vma=False,
    )
```

```python
import functools
import math
import jax
import jax.numpy as jnp
from jax import lax
from jax.experimental import pallas as pl
from jax.experimental.pallas import tpu as pltpu
from jax.sharding import PartitionSpec as P

FINE = lax.Precision.HIGHEST
MERGE_BYTES = 24 << 20
f32, bf16 = jnp.float32, jnp.bfloat16
ANYWHERE = -2


def pair_number(higher, lower_level):
    return higher * (higher - 1) // 2 + lower_level


def times_transposed(v, g, precision=None):
    return lax.dot_general(
        v, g, (((1,), (1,)), ((), ())), precision=precision, preferred_element_type=f32
    )


def times(v, g, precision=None):
    return lax.dot_general(
        v, g, (((1,), (0,)), ((), ())), precision=precision, preferred_element_type=f32
    )


def split_product(d, g):
    high = d.astype(bf16)
    low = (d - high.astype(f32)).astype(bf16)
    return times(high, g) + times(low, g)


def kernel_call(body, ins, outs, scratch=None):
    in_keys, out_keys, scratch = list(ins), list(outs), scratch or {}
    arrays, specs, held = [], [], 0
    for value in ins.values():
        array, at = value if isinstance(value, tuple) else (value, -1)
        if array.dtype == jnp.int32:
            specs.append(pl.BlockSpec(memory_space=pltpu.SMEM))
        elif at is None:
            array = pltpu.with_memory_space_constraint(array, pltpu.HBM)
            specs.append(pl.BlockSpec(memory_space=pltpu.HBM))
        else:
            shape = array.shape
            if at >= 0:
                shape = (1,) + shape[1:]
            if at > -2:
                array = pltpu.with_memory_space_constraint(array, pltpu.HBM)
            index = (max(at, 0),) + (0,) * (len(shape) - 1)
            specs.append(pl.BlockSpec(shape, lambda *_, index=index: index))
            held += math.prod(shape) * array.dtype.itemsize
        arrays.append(array)
    shapes = list(outs.values())
    if len(shapes) == 1:
        shapes.append(((8, 128), f32))
    held += sum(math.prod(s[0]) * jnp.dtype(s[1]).itemsize for s in shapes)

    def kernel(*refs):
        spare = [None] * (len(shapes) - len(out_keys))
        body(dict(zip(in_keys + out_keys + spare + list(scratch), refs)))
        if spare:
            last = refs[len(in_keys) + 1]
            last[...] = jnp.zeros(last.shape, f32)

    values = pl.pallas_call(
        kernel,
        grid=(1,),
        out_shape=[(pltpu.VMEM if len(s) > 2 else pltpu.HBM)(s[0], s[1]) for s in shapes],
        in_specs=specs,
        out_specs=[pl.BlockSpec(s[0], lambda *_, d=len(s[0]): (0,) * d) for s in shapes],
        scratch_shapes=[pltpu.VMEM(*s) for s in scratch.values()],
        compiler_params=pltpu.CompilerParams(vmem_limit_bytes=2 * held + (4 << 20)),
    )(*arrays)
    return dict(zip(out_keys, values))


def exchange(value, step, size):
    return lax.ppermute(value, "col", [(c, c ^ step) for c in range(size)])


def shards(rows, cols, right_side, inverses, factor_blocks, pattern):
    return body_of(rows, cols, right_side, inverses, factor_blocks, pattern)


def body_of(rows, cols, right_side, inverses, factor_blocks, pattern):
    levels, _, rhs, depth = right_side.shape
    width = factor_blocks.shape[2]
    chunk = rhs // cols
    top = levels - 1
    col = lax.axis_index("col").reshape(1).astype(jnp.int32)
    row = lax.axis_index("row").reshape(1).astype(jnp.int32)
    panel, sent = (chunk, depth), (rows, chunk, depth)
    block = depth * depth * factor_blocks.dtype.itemsize
    sizes = factor_blocks.shape[0] * cols * width * block + 6 * rows * width * block
    merging = sizes <= MERGE_BYTES and levels % 2 == 0 and rows & (rows - 1) == 0
    merged = range(0, top - 1, 2) if merging else ()
    steps = [1 << s for s in reversed(range((cols - 1).bit_length()))]

    COL, ROW, PATTERN, BLOCKS, WAIT, ARRIVED, CARRY, SEND, OUT, ALL = range(10)
    INV, RIGHT, PANEL, X, Y, V, _, FAR = range(10, 18)

    def inv(*ms):
        return {(INV, m): (inverses, m) for m in ms}

    def right(m):
        return {(RIGHT, m): (right_side, m)}

    def own(r, m):
        return r[RIGHT, m][0, 0, pl.ds(pl.multiple_of(r[COL][0] * chunk, chunk), chunk), :]

    def swap(value):
        return lax.all_to_all(value, "row", 0, 0)

    def send_all(r, value):
        for k in range(rows):
            r[SEND][k] = value

    cuts = [(1, 2), (2, 4), (4, levels)]
    bundles = {n: [(m, l) for m in range(*cut) for l in range(m)] for n, cut in zip("abc", cuts)}
    place = {pair: (n, s) for n, pairs in bundles.items() for s, pair in enumerate(pairs)}
    held, arrays = {}, {}

    def near(name, q):
        return merging and q > 0 and name in "bcd"

    def shape_of(pairs):
        return (len(pairs), width, depth, depth), bf16

    def add_bundle(name):
        found = {0: held[name]}
        if name == "a":
            found |= {q: exchange(held[name], q, cols) for q in range(cols - 1, 0, -1)}
        for step in steps if name != "a" else ():
            found |= {q ^ step: exchange(v, step, cols) for q, v in found.items()}
        for q, v in found.items():
            arrays[name, q] = pltpu.with_memory_space_constraint(v, pltpu.VMEM) if near(name, q) else v

    def need(*keys):
        found = {}
        for n, s in sorted({place[k] for k in keys}):
            for q in range(cols):
                v = arrays[n, q]
                if near(n, q):
                    found[n, q] = (v, ANYWHERE)
                else:
                    found[n, s, q] = (v, ANYWHERE if v.shape[0] == 1 else s)
        return found

    def groups(r, key):
        name, s = place[key]
        return [r[name, q].at[s] if near(name, q) else r[name, s, q].at[0] for q in range(cols)]

    def column(r, q, j):
        return (r[COL][0] ^ q) * width + j

    def sum_over(r, m, lower):
        total = None
        for l in lower:
            for q, blocks in enumerate(groups(r, (m, l))):
                for j in range(0, width, 2):
                    pair = range(j, min(j + 2, width))
                    term = times_transposed(
                        jnp.concatenate([r[PANEL, l][column(r, q, i)] for i in pair], 1),
                        jnp.concatenate([blocks[i] for i in pair], 1),
                    )
                    total = term if total is None else total + term
        return total

    def spread_sums(r, terms, out_ref, slot, carried=None):
        for q in range(cols):
            for j in range(0, width, 2):
                pair = range(j, min(j + 2, width))
                total = None
                for value, key in terms:
                    blocks = groups(r, key)[q]
                    term = times(value, jnp.concatenate([blocks[i] for i in pair], 1))
                    total = term if total is None else total + term
                for s, i in enumerate(pair):
                    k = column(r, q, i)
                    part = total[:, s * depth : (s + 1) * depth]
                    if carried is not None:
                        part = part + carried[k, slot]
                    out_ref[k, slot] = part.astype(out_ref.dtype)

    def masked(r, p, at, j):
        value = r[BLOCKS][at, 0, j]
        return jnp.where(r[PATTERN][p, 0, j] != 0, value, jnp.zeros_like(value))

    def first_body(r):
        value = times_transposed(own(r, 0), r[INV, 0][0, 0], FINE)
        r[X][...] = value
        send_all(r, value.astype(bf16))
        for j in range(width):
            r[OUT][0, j] = masked(r, 0, 0, j)

    out = kernel_call(
        first_body,
        {COL: col, PATTERN: pattern, BLOCKS: (factor_blocks, 0), **right(0), **inv(0)},
        {X: (panel, f32), SEND: (sent, bf16), OUT: shape_of("a")},
    )
    x = {0: out[X]}
    held["a"] = out[OUT]

    def mask_body(r):
        for name, pairs in bundles.items():
            for s, (m, l) in enumerate(pairs):
                for j in range(width):
                    value = masked(r, pair_number(m, l), pair_number(m, l), j)
                    if name in r:
                        r[name][s, j] = value
                    if l in merged and m == l + 1:
                        product = split_product(r[INV, m][0, 0], value)
                        r[OUT][l // 2, :, j * depth : (j + 1) * depth] = product.astype(bf16)

    outs = {n: shape_of(pairs) for n, pairs in bundles.items() if n != "a"}
    if merged:
        outs[OUT] = ((len(merged), depth, width * depth), bf16)
    found = kernel_call(
        mask_body,
        {PATTERN: pattern, BLOCKS: factor_blocks, WAIT: (out[SEND], None), **inv(*[l + 1 for l in merged])}, outs,
    )
    product = found.pop(OUT, None)
    held |= found
    for name in bundles:
        add_bundle(name)

    products = {0: product}
    if merged:
        for d in [1 << s for s in reversed(range((rows - 1).bit_length()))]:
            products |= {s ^ d: lax.ppermute(v, "row", [(r, r ^ d) for r in range(rows)]) for s, v in products.items()}

    gathered = {0: (swap(out[SEND]), ANYWHERE)}
    y, rounded = {}, {}

    def panels(lower):
        return {(PANEL, l): gathered[l] for l in lower}

    for m in range(1, levels):
        def solve_body(r):
            value = times_transposed(own(r, m) - sum_over(r, m, range(m)), r[INV, m][0, 0], FINE)
            r[X][...] = value
            if m < top:
                send_all(r, value.astype(bf16))
                return
            result = times(value, r[INV, m][0, 0], FINE)
            r[Y][...] = result
            r[V][...] = result.astype(bf16)
            spread_sums(r, [(result.astype(bf16), (m, m - 1))], r[SEND], 0)

        outs = {X: (panel, f32), SEND: (sent, bf16)}
        if m == top:
            outs = {X: (panel, f32), Y: (panel, f32), V: (panel, bf16), SEND: ((rows, 1, chunk, depth), bf16)}
        out = kernel_call(
            solve_body,
            {COL: col, **right(m), **inv(m), **panels(range(m)), **need(*[(m, l) for l in range(m)])}, outs,
        )
        x[m] = out[X]
        if m < top:
            gathered[m] = (swap(out[SEND]), ANYWHERE)
    y[top], rounded[top] = out[Y], out[V]

    wanted = [(m, l) for l in reversed(merged) for m in range(l + 2, levels)]
    if merged:
        first = [key for key in wanted if key[1] == merged[-1]]
        fixed = {"d": first, "g": wanted[len(first) :]}

        def fix_body(r):
            for s in range(rows):
                r[ALL][r[ROW][0] ^ s] = r[FAR, s][...]
            for n, s, m, l in [(n, s, *key) for n, keys in fixed.items() for s, key in enumerate(keys)]:
                total = None
                for q, blocks in enumerate(groups(r, (m, l + 1))):
                    for j in range(width):
                        term = times(blocks[j], r[ALL][column(r, q, j), l // 2])
                        total = term if total is None else total + term
                for j in range(width):
                    raw = groups(r, (m, l))[0][j].astype(f32)
                    r[n][s, j] = (raw - total[:, j * depth : (j + 1) * depth]).astype(bf16)

        held |= kernel_call(
            fix_body,
            {COL: col, ROW: row, **{(FAR, s): (v, ANYWHERE) for s, v in products.items()}}
            | need(*wanted, *[(m, l + 1) for m, l in wanted]),
            {n: shape_of(keys) for n, keys in fixed.items()}, {ALL: ((rows,) + product.shape, bf16)},
        )
        for n, keys in fixed.items():
            add_bundle(n)
            for s, (m, l) in enumerate(keys):
                place[m, l, True] = (n, s)

    lower = [(l, l + 1) for l in reversed(merged)] if merged else [(l,) for l in range(top - 2, -1, -1)]
    plan = [(top - 1,)] + lower

    def terms_for(l, values):
        return [(v, (m, l, True) if (m, l) in wanted else (m, l)) for m, v in values.items()]

    def pairs_for(targets, upper):
        return need(*[key for l in targets for _, key in terms_for(l, dict.fromkeys(upper))])

    for s, done in enumerate(plan):
        targets = plan[s + 1] if s + 1 < len(plan) else ()
        upper = range(done[-1] + 1, levels)
        arrived = (swap(out[SEND]), ANYWHERE)
        slots = (rows, max(len(targets), 1), chunk, depth)
        ins = {COL: col, ARRIVED: arrived, **inv(*done), **{(X, m): x[m] for m in done}}
        if targets:
            odds = [l + 1 for l in targets if l in merged]

            def carry_terms(r):
                values = {m: r[V, m][...] for m in upper}
                terms = {l: terms_for(l, values) for l in targets}
                for m in odds:
                    own_part = times(r[X, m][...], r[INV, m][0, 0], FINE).astype(bf16)
                    terms[m - 1].append((own_part, (m, m - 1)))
                return terms

            known = {(V, m): rounded[m] for m in upper} | {(X, m): x[m] for m in odds} | inv(*odds)
            known |= pairs_for(targets, upper) | need(*[(m, m - 1) for m in odds])
            if s > 0:
                def carry_body(r):
                    for slot, (l, terms) in enumerate(carry_terms(r).items()):
                        spread_sums(r, terms, r[CARRY], slot)

                known = kernel_call(carry_body, {COL: col, **known}, {CARRY: (slots, f32)})
            ins |= {**known, **pairs_for(targets, done)}

        def step_body(r):
            values = {}
            for slot, m in enumerate(done):
                total = r[ARRIVED][0, slot].astype(f32)
                for k in range(1, rows):
                    total = total + r[ARRIVED][k, slot].astype(f32)
                result = times(r[X, m][...] - total, r[INV, m][0, 0], FINE)
                if not targets:
                    r[OUT][slot] = result
                    continue
                r[Y, m][...] = result
                values[m] = result.astype(bf16)
                r[V, m][...] = values[m]
            folded = carry_terms(r) if targets and s == 0 else {}
            for slot, l in enumerate(targets):
                spread_sums(r, terms_for(l, values) + folded.get(l, []), r[SEND], slot, r.get(CARRY))

        if targets:
            outs = {(Y, m): (panel, f32) for m in done} | {(V, m): (panel, bf16) for m in done} | {SEND: (slots, bf16)}
        else:
            outs = {OUT: ((len(done),) + panel, f32)}
        out = kernel_call(step_body, ins, outs)
        if targets:
            for m in done:
                y[m], rounded[m] = out[Y, m], out[V, m]

    def pieces(value):
        found = {q: exchange(value, q, cols) for q in range(cols - 1, 0, -1)}
        return [value] + [found[q] for q in range(1, cols)]

    def stacked(values):
        def stack_body(r):
            for s in range(len(values)):
                r[OUT][s] = r[X, s][...]

        return kernel_call(
            stack_body, {(X, s): v for s, v in enumerate(values)}, {OUT: ((len(values),) + panel, f32)}
        )[OUT]

    def joined(*runs):
        def join_body(r):
            at = 0
            for s, run in enumerate(runs):
                count = run[0].shape[0]
                for q in range(cols):
                    where = pl.ds(pl.multiple_of((r[COL][0] ^ q) * chunk, chunk), chunk)
                    r[OUT][pl.ds(at, count), where, :] = r[X, s, q][...]
                at += count

        ins = {(X, s, q): (v, ANYWHERE if q else -1) for s, run in enumerate(runs) for q, v in enumerate(run)}
        return kernel_call(join_body, {COL: col, **ins}, {OUT: ((levels, rhs, depth), f32)})[OUT][:, None]

    high = pieces(stacked([y[m] for m in range(len(plan[-1]), levels)]))
    forward = joined(pieces(stacked([x[m] for m in range(levels)])))
    return forward, joined(pieces(out[OUT]), high)


def solution(mesh):
    rows, cols = mesh.shape["row"], mesh.shape["col"]
    placed = (
        P(None, "row", None, None),
        P(None, "row", None, None),
        P(None, "row", "col", None, None),
        P(None, "row", "col"),
    )
    return jax.shard_map(
        functools.partial(shards, rows, cols),
        mesh=mesh,
        in_specs=placed,
        out_specs=(P(None, "row", None, None), P(None, "row", None, None)),
        check_vma=False,
    )
```

```python
import functools
import math
import jax
import jax.numpy as jnp
from jax import lax
from jax.experimental import pallas as pl
from jax.experimental.pallas import tpu as pltpu
from jax.sharding import PartitionSpec as P

FINE = lax.Precision.HIGHEST
MERGE_BYTES = 24 << 20
f32, bf16 = jnp.float32, jnp.bfloat16
ANYWHERE = -2


def pair_number(higher, lower_level):
    return higher * (higher - 1) // 2 + lower_level


def times_transposed(v, g, precision=None):
    return lax.dot_general(
        v, g, (((1,), (1,)), ((), ())), precision=precision, preferred_element_type=f32
    )


def times(v, g, precision=None):
    return lax.dot_general(
        v, g, (((1,), (0,)), ((), ())), precision=precision, preferred_element_type=f32
    )


def split_product(d, g):
    high = d.astype(bf16)
    low = (d - high.astype(f32)).astype(bf16)
    return times(high, g) + times(low, g)


def kernel_call(body, ins, outs, scratch=None):
    in_keys, out_keys, scratch = list(ins), list(outs), scratch or {}
    arrays, specs, held = [], [], 0
    for value in ins.values():
        array, at = value if isinstance(value, tuple) else (value, -1)
        if array.dtype == jnp.int32:
            if array.size > 1:
                array = pltpu.with_memory_space_constraint(array, pltpu.HBM)
            specs.append(pl.BlockSpec(memory_space=pltpu.SMEM))
        elif at is None:
            array = pltpu.with_memory_space_constraint(array, pltpu.HBM)
            specs.append(pl.BlockSpec(memory_space=pltpu.HBM))
        else:
            shape = array.shape
            if at >= 0:
                shape = (1,) + shape[1:]
            if at > -2:
                array = pltpu.with_memory_space_constraint(array, pltpu.HBM)
            index = (max(at, 0),) + (0,) * (len(shape) - 1)
            specs.append(pl.BlockSpec(shape, lambda *_, index=index: index))
            held += math.prod(shape) * array.dtype.itemsize
        arrays.append(array)
    shapes = list(outs.values())
    if len(shapes) == 1:
        shapes.append(((8, 128), f32))
    held += sum(math.prod(s[0]) * jnp.dtype(s[1]).itemsize for s in shapes)

    def kernel(*refs):
        spare = [None] * (len(shapes) - len(out_keys))
        body(dict(zip(in_keys + out_keys + spare + list(scratch), refs)))
        if spare:
            last = refs[len(in_keys) + 1]
            last[...] = jnp.zeros(last.shape, f32)

    values = pl.pallas_call(
        kernel,
        grid=(1,),
        out_shape=[(pltpu.VMEM if len(s) > 2 else pltpu.HBM)(s[0], s[1]) for s in shapes],
        in_specs=specs,
        out_specs=[pl.BlockSpec(s[0], lambda *_, d=len(s[0]): (0,) * d) for s in shapes],
        scratch_shapes=[pltpu.VMEM(*s) for s in scratch.values()],
        compiler_params=pltpu.CompilerParams(vmem_limit_bytes=2 * held + (4 << 20)),
    )(*arrays)
    return dict(zip(out_keys, values))


def exchange(value, step, size):
    return lax.ppermute(value, "col", [(c, c ^ step) for c in range(size)])


def shards(rows, cols, right_side, inverses, factor_blocks, pattern):
    return body_of(rows, cols, right_side, inverses, factor_blocks, pattern)


def body_of(rows, cols, right_side, inverses, factor_blocks, pattern):
    levels, _, rhs, depth = right_side.shape
    width = factor_blocks.shape[2]
    chunk = rhs // cols
    top = levels - 1
    pattern = jnp.transpose(pattern, (1, 2, 0))
    col = lax.axis_index("col").reshape(1).astype(jnp.int32)
    row = lax.axis_index("row").reshape(1).astype(jnp.int32)
    panel, sent = (chunk, depth), (rows, chunk, depth)
    block = depth * depth * factor_blocks.dtype.itemsize
    sizes = factor_blocks.shape[0] * cols * width * block + 6 * rows * width * block
    merging = sizes <= MERGE_BYTES and levels % 2 == 0 and rows & (rows - 1) == 0
    merged = range(0, top - 1, 2) if merging else ()
    steps = [1 << s for s in reversed(range((cols - 1).bit_length()))]

    COL, ROW, PATTERN, BLOCKS, WAIT, ARRIVED, CARRY, SEND, OUT, ALL, STACK = range(11)
    INV, RIGHT, PANEL, X, Y, V, FAR = range(11, 18)

    def inv(*ms):
        return {(INV, m): (inverses, m) for m in ms}

    def right(m):
        return {(RIGHT, m): (right_side, m)}

    def own(r, m):
        return r[RIGHT, m][0, 0, pl.ds(pl.multiple_of(r[COL][0] * chunk, chunk), chunk), :]

    def swap(value):
        return lax.all_to_all(value, "row", 0, 0)

    def send_all(r, value):
        for k in range(rows):
            r[SEND][k] = value

    cuts = [(1, 2), (2, 4), (4, levels)]
    bundles = {n: [(m, l) for m in range(*cut) for l in range(m)] for n, cut in zip("abc", cuts)}
    place = {pair: (n, s) for n, pairs in bundles.items() for s, pair in enumerate(pairs)}
    held, arrays = {}, {}

    def near(name, q):
        return merging and q > 0 and name in "bcd"

    def shape_of(pairs):
        return (len(pairs), width, depth, depth), bf16

    def add_bundle(name):
        found = {0: held[name]}
        if name == "a":
            found |= {q: exchange(held[name], q, cols) for q in range(cols - 1, 0, -1)}
        for step in steps if name != "a" else ():
            found |= {q ^ step: exchange(v, step, cols) for q, v in found.items()}
        for q, v in found.items():
            arrays[name, q] = pltpu.with_memory_space_constraint(v, pltpu.VMEM) if near(name, q) else v

    def need(*keys):
        found = {}
        for n, s in sorted({place[k] for k in keys}):
            for q in range(cols):
                v = arrays[n, q]
                if near(n, q):
                    found[n, q] = (v, ANYWHERE)
                else:
                    found[n, s, q] = (v, ANYWHERE if v.shape[0] == 1 else s)
        return found

    def groups(r, key):
        name, s = place[key]
        return [r[name, q].at[s] if near(name, q) else r[name, s, q].at[0] for q in range(cols)]

    def column(r, q, j):
        return (r[COL][0] ^ q) * width + j

    def sum_over(r, m, lower):
        total = None
        for l in lower:
            for q, blocks in enumerate(groups(r, (m, l))):
                for j in range(0, width, 2):
                    pair = range(j, min(j + 2, width))
                    term = times_transposed(
                        jnp.concatenate([r[PANEL, l][column(r, q, i)] for i in pair], 1),
                        jnp.concatenate([blocks[i] for i in pair], 1),
                    )
                    total = term if total is None else total + term
        return total

    def spread_sums(r, terms, out_ref, slot, carried=None):
        for q in range(cols):
            for j in range(0, width, 2):
                pair = range(j, min(j + 2, width))
                total = None
                for value, key in terms:
                    blocks = groups(r, key)[q]
                    term = times(value, jnp.concatenate([blocks[i] for i in pair], 1))
                    total = term if total is None else total + term
                for s, i in enumerate(pair):
                    k = column(r, q, i)
                    part = total[:, s * depth : (s + 1) * depth]
                    if carried is not None:
                        part = part + carried[k, slot]
                    out_ref[k, slot] = part.astype(out_ref.dtype)

    def masked(r, p, at, j):
        value = r[BLOCKS][at, 0, j]
        return jnp.where(r[PATTERN][0, j, p] != 0, value, jnp.zeros_like(value))

    def first_body(r):
        value = times_transposed(own(r, 0), r[INV, 0][0, 0], FINE)
        r[X][...] = value
        send_all(r, value.astype(bf16))
        for j in range(width):
            r[OUT][0, j] = masked(r, 0, 0, j)

    out = kernel_call(
        first_body,
        {COL: col, PATTERN: pattern, BLOCKS: (factor_blocks, 0), **right(0), **inv(0)},
        {X: (panel, f32), SEND: (sent, bf16), OUT: shape_of("a")},
    )
    x = {0: out[X]}
    held["a"] = out[OUT]

    def mask_body(r):
        for name, pairs in bundles.items():
            for s, (m, l) in enumerate(pairs):
                for j in range(width):
                    value = masked(r, pair_number(m, l), pair_number(m, l), j)
                    if name in r:
                        r[name][s, j] = value
                    if l in merged and m == l + 1:
                        product = split_product(r[INV, m][0, 0], value)
                        r[OUT][l // 2, :, j * depth : (j + 1) * depth] = product.astype(bf16)

    outs = {n: shape_of(pairs) for n, pairs in bundles.items() if n != "a"}
    if merged:
        outs[OUT] = ((len(merged), depth, width * depth), bf16)
    found = kernel_call(
        mask_body,
        {PATTERN: pattern, BLOCKS: factor_blocks, WAIT: (out[SEND], None), **inv(*[l + 1 for l in merged])}, outs,
    )
    product = found.pop(OUT, None)
    held |= found
    for name in bundles:
        add_bundle(name)

    products = {0: product}
    if merged:
        for d in [1 << s for s in reversed(range((rows - 1).bit_length()))]:
            products |= {s ^ d: lax.ppermute(v, "row", [(r, r ^ d) for r in range(rows)]) for s, v in products.items()}

    gathered = {0: (swap(out[SEND]), ANYWHERE)}
    y, rounded = {}, {}

    def panels(lower):
        return {(PANEL, l): gathered[l] for l in lower}

    for m in range(1, levels):
        def solve_body(r):
            value = times_transposed(own(r, m) - sum_over(r, m, range(m)), r[INV, m][0, 0], FINE)
            if m < top:
                r[X][...] = value
                send_all(r, value.astype(bf16))
                return
            for l in range(top):
                r[STACK][l] = r[X, l][...]
            r[STACK][top] = value
            result = times(value, r[INV, m][0, 0], FINE)
            r[Y][...] = result
            r[V][...] = result.astype(bf16)
            spread_sums(r, [(result.astype(bf16), (m, m - 1))], r[SEND], 0)

        outs = {X: (panel, f32), SEND: (sent, bf16)}
        if m == top:
            outs = {STACK: ((levels,) + panel, f32), Y: (panel, f32), V: (panel, bf16)}
            outs |= {SEND: ((rows, 1, chunk, depth), bf16)}
        out = kernel_call(
            solve_body,
            {COL: col, **right(m), **inv(m), **panels(range(m)), **need(*[(m, l) for l in range(m)])}
            | {(X, l): x[l] for l in range(top) if m == top}, outs,
        )
        if m < top:
            x[m] = out[X]
            gathered[m] = (swap(out[SEND]), ANYWHERE)
    y[top], rounded[top] = out[Y], out[V]
    solved = out[STACK]

    wanted = [(m, l) for l in reversed(merged) for m in range(l + 2, levels)]
    if merged:
        first = [key for key in wanted if key[1] == merged[-1]]
        fixed = {"d": first, "g": wanted[len(first) :]}

        def fix_body(r):
            for s in range(rows):
                r[ALL][r[ROW][0] ^ s] = r[FAR, s][...]
            for n, s, m, l in [(n, s, *key) for n, keys in fixed.items() for s, key in enumerate(keys)]:
                total = None
                for q, blocks in enumerate(groups(r, (m, l + 1))):
                    for j in range(width):
                        term = times(blocks[j], r[ALL][column(r, q, j), l // 2])
                        total = term if total is None else total + term
                for j in range(width):
                    raw = groups(r, (m, l))[0][j].astype(f32)
                    r[n][s, j] = (raw - total[:, j * depth : (j + 1) * depth]).astype(bf16)

        held |= kernel_call(
            fix_body,
            {COL: col, ROW: row, **{(FAR, s): (v, ANYWHERE) for s, v in products.items()}}
            | need(*wanted, *[(m, l + 1) for m, l in wanted]),
            {n: shape_of(keys) for n, keys in fixed.items()}, {ALL: ((rows,) + product.shape, bf16)},
        )
        for n, keys in fixed.items():
            add_bundle(n)
            for s, (m, l) in enumerate(keys):
                place[m, l, True] = (n, s)

    lower = [(l, l + 1) for l in reversed(merged)] if merged else [(l,) for l in range(top - 2, -1, -1)]
    plan = [(top - 1,)] + lower

    def terms_for(l, values):
        return [(v, (m, l, True) if (m, l) in wanted else (m, l)) for m, v in values.items()]

    def pairs_for(targets, upper):
        return need(*[key for l in targets for _, key in terms_for(l, dict.fromkeys(upper))])

    for s, done in enumerate(plan):
        targets = plan[s + 1] if s + 1 < len(plan) else ()
        upper = range(done[-1] + 1, levels)
        stacks = s + 2 == len(plan)
        arrived = (swap(out[SEND]), ANYWHERE)
        slots = (rows, max(len(targets), 1), chunk, depth)
        ins = {COL: col, ARRIVED: arrived, **inv(*done), **{(X, m): x[m] for m in done}}
        if targets:
            odds = [l + 1 for l in targets if l in merged]

            def carry_terms(r):
                values = {m: r[V, m][...] for m in upper}
                terms = {l: terms_for(l, values) for l in targets}
                for m in odds:
                    own_part = times(r[X, m][...], r[INV, m][0, 0], FINE).astype(bf16)
                    terms[m - 1].append((own_part, (m, m - 1)))
                return terms

            known = {(V, m): rounded[m] for m in upper} | {(X, m): x[m] for m in odds} | inv(*odds)
            known |= pairs_for(targets, upper) | need(*[(m, m - 1) for m in odds])
            if s > 0:
                def carry_body(r):
                    for slot, (l, terms) in enumerate(carry_terms(r).items()):
                        spread_sums(r, terms, r[CARRY], slot)

                known = kernel_call(carry_body, {COL: col, **known}, {CARRY: (slots, f32)})
            ins |= {**known, **pairs_for(targets, done)}

        def step_body(r):
            values = {}
            for slot, m in enumerate(done):
                total = r[ARRIVED][0, slot].astype(f32)
                for k in range(1, rows):
                    total = total + r[ARRIVED][k, slot].astype(f32)
                result = times(r[X, m][...] - total, r[INV, m][0, 0], FINE)
                if not targets:
                    r[OUT][slot] = result
                    continue
                if stacks:
                    r[STACK][m - len(targets)] = result
                else:
                    r[Y, m][...] = result
                values[m] = result.astype(bf16)
                r[V, m][...] = values[m]
            for m in upper if stacks else ():
                r[STACK][m - len(targets)] = r[Y, m][...]
            folded = carry_terms(r) if targets and s == 0 else {}
            for slot, l in enumerate(targets):
                spread_sums(r, terms_for(l, values) + folded.get(l, []), r[SEND], slot, r.get(CARRY))

        if targets:
            outs = {(V, m): (panel, bf16) for m in done} | {SEND: (slots, bf16)}
            if stacks:
                outs[STACK] = ((levels - len(targets),) + panel, f32)
                ins |= {(Y, m): y[m] for m in upper}
            else:
                outs |= {(Y, m): (panel, f32) for m in done}
        else:
            outs = {OUT: ((len(done),) + panel, f32)}
        out = kernel_call(step_body, ins, outs)
        if targets:
            for m in done:
                y[m], rounded[m] = out.get((Y, m)), out[V, m]
            high = out.get(STACK)

    def pieces(value):
        found = {q: exchange(value, q, cols) for q in range(cols - 1, 0, -1)}
        return [value] + [found[q] for q in range(1, cols)]

    def joined(*runs):
        def join_body(r):
            at = 0
            for s, run in enumerate(runs):
                count = run[0].shape[0]
                for q in range(cols):
                    where = pl.ds(pl.multiple_of((r[COL][0] ^ q) * chunk, chunk), chunk)
                    r[OUT][pl.ds(at, count), where, :] = r[X, s, q][...]
                at += count

        ins = {(X, s, q): (v, ANYWHERE if q else -1) for s, run in enumerate(runs) for q, v in enumerate(run)}
        return kernel_call(join_body, {COL: col, **ins}, {OUT: ((levels, rhs, depth), f32)})[OUT][:, None]

    last = pieces(out[OUT])
    forward = joined(pieces(solved))
    return forward, joined(last, pieces(high))


def solution(mesh):
    rows, cols = mesh.shape["row"], mesh.shape["col"]
    placed = (
        P(None, "row", None, None),
        P(None, "row", None, None),
        P(None, "row", "col", None, None),
        P(None, "row", "col"),
    )
    return jax.shard_map(
        functools.partial(shards, rows, cols),
        mesh=mesh,
        in_specs=placed,
        out_specs=(P(None, "row", None, None), P(None, "row", None, None)),
        check_vma=False,
    )
```

```python
import functools
import math
import jax
import jax.numpy as jnp
from jax import lax
from jax.experimental import pallas as pl
from jax.experimental.pallas import tpu as pltpu
from jax.sharding import PartitionSpec as P

FINE = lax.Precision.HIGHEST
MERGE_BYTES = 24 << 20
f32, bf16 = jnp.float32, jnp.bfloat16
ANYWHERE = -2


def pair_number(higher, lower_level):
    return higher * (higher - 1) // 2 + lower_level


def times_transposed(v, g, precision=None):
    return lax.dot_general(
        v, g, (((1,), (1,)), ((), ())), precision=precision, preferred_element_type=f32
    )


def times(v, g, precision=None):
    return lax.dot_general(
        v, g, (((1,), (0,)), ((), ())), precision=precision, preferred_element_type=f32
    )


def split_product(d, g):
    high = d.astype(bf16)
    low = (d - high.astype(f32)).astype(bf16)
    return times(high, g) + times(low, g)


def kernel_call(body, ins, outs, scratch=None):
    in_keys, out_keys, scratch = list(ins), list(outs), scratch or {}
    arrays, specs, held = [], [], 0
    for value in ins.values():
        array, at = value if isinstance(value, tuple) else (value, -1)
        if array.dtype == jnp.int32:
            if array.size > 1:
                array = pltpu.with_memory_space_constraint(array, pltpu.HBM)
            specs.append(pl.BlockSpec(memory_space=pltpu.SMEM))
        elif at is None:
            array = pltpu.with_memory_space_constraint(array, pltpu.HBM)
            specs.append(pl.BlockSpec(memory_space=pltpu.HBM))
        else:
            shape = array.shape
            if at >= 0:
                shape = (1,) + shape[1:]
            if at > -2:
                array = pltpu.with_memory_space_constraint(array, pltpu.HBM)
            index = (max(at, 0),) + (0,) * (len(shape) - 1)
            specs.append(pl.BlockSpec(shape, lambda *_, index=index: index))
            held += math.prod(shape) * array.dtype.itemsize
        arrays.append(array)
    shapes = list(outs.values())
    if len(shapes) == 1:
        shapes.append(((8, 128), f32))
    held += sum(math.prod(s[0]) * jnp.dtype(s[1]).itemsize for s in shapes)

    def kernel(*refs):
        spare = [None] * (len(shapes) - len(out_keys))
        body(dict(zip(in_keys + out_keys + spare + list(scratch), refs)))
        if spare:
            last = refs[len(in_keys) + 1]
            last[...] = jnp.zeros(last.shape, f32)

    values = pl.pallas_call(
        kernel,
        grid=(1,),
        out_shape=[(pltpu.VMEM if len(s) > 2 else pltpu.HBM)(s[0], s[1]) for s in shapes],
        in_specs=specs,
        out_specs=[pl.BlockSpec(s[0], lambda *_, d=len(s[0]): (0,) * d) for s in shapes],
        scratch_shapes=[pltpu.VMEM(*s) for s in scratch.values()],
        compiler_params=pltpu.CompilerParams(vmem_limit_bytes=2 * held + (4 << 20)),
    )(*arrays)
    return dict(zip(out_keys, values))


def exchange(value, step, size):
    return lax.ppermute(value, "col", [(c, c ^ step) for c in range(size)])


def shards(rows, cols, right_side, inverses, factor_blocks, pattern):
    return body_of(rows, cols, right_side, inverses, factor_blocks, pattern)


def body_of(rows, cols, right_side, inverses, factor_blocks, pattern):
    levels, _, rhs, depth = right_side.shape
    width = factor_blocks.shape[2]
    chunk = rhs // cols
    top = levels - 1
    pattern = jnp.transpose(pattern, (1, 2, 0))
    col = lax.axis_index("col").reshape(1).astype(jnp.int32)
    row = lax.axis_index("row").reshape(1).astype(jnp.int32)
    panel, sent = (chunk, depth), (rows, chunk, depth)
    block = depth * depth * factor_blocks.dtype.itemsize
    sizes = factor_blocks.shape[0] * cols * width * block + 6 * rows * width * block
    merging = sizes <= MERGE_BYTES and levels % 2 == 0 and rows & (rows - 1) == 0
    merged = range(0, top - 1, 2) if merging else ()
    steps = [1 << s for s in reversed(range((cols - 1).bit_length()))]

    COL, ROW, PATTERN, BLOCKS, WAIT, ARRIVED, CARRY, SEND, OUT, ALL, STACK = range(11)
    INV, RIGHT, PANEL, X, Y, V, FAR = range(11, 18)

    def inv(*ms):
        return {(INV, m): (inverses, m) for m in ms}

    def right(m):
        return {(RIGHT, m): (right_side, m)}

    def own(r, m):
        return r[RIGHT, m][0, 0, pl.ds(pl.multiple_of(r[COL][0] * chunk, chunk), chunk), :]

    def swap(value):
        return lax.all_to_all(value, "row", 0, 0)

    def send_all(r, value):
        for k in range(rows):
            r[SEND][k] = value

    cuts = [(1, 2), (2, 4), (4, levels)]
    bundles = {n: [(m, l) for m in range(*cut) for l in range(m)] for n, cut in zip("abc", cuts)}
    place = {pair: (n, s) for n, pairs in bundles.items() for s, pair in enumerate(pairs)}
    held, arrays = {}, {}

    def near(name, q):
        return merging and q > 0 and name in "bcd"

    def shape_of(pairs):
        return (len(pairs), width, depth, depth), bf16

    def add_bundle(name):
        found = {0: held[name]}
        if name == "a":
            found |= {q: exchange(held[name], q, cols) for q in range(cols - 1, 0, -1)}
        for step in steps if name != "a" else ():
            found |= {q ^ step: exchange(v, step, cols) for q, v in found.items()}
        for q, v in found.items():
            arrays[name, q] = pltpu.with_memory_space_constraint(v, pltpu.VMEM) if near(name, q) else v

    def need(*keys):
        found = {}
        for n, s in sorted({place[k] for k in keys}):
            for q in range(cols):
                v = arrays[n, q]
                if near(n, q):
                    found[n, q] = (v, ANYWHERE)
                else:
                    found[n, s, q] = (v, ANYWHERE if v.shape[0] == 1 else s)
        return found

    def groups(r, key):
        name, s = place[key]
        return [r[name, q].at[s] if near(name, q) else r[name, s, q].at[0] for q in range(cols)]

    def column(r, q, j):
        return (r[COL][0] ^ q) * width + j

    def sum_over(r, m, lower):
        total = None
        for l in lower:
            for q, blocks in enumerate(groups(r, (m, l))):
                for j in range(0, width, 2):
                    pair = range(j, min(j + 2, width))
                    term = times_transposed(
                        jnp.concatenate([r[PANEL, l][column(r, q, i)] for i in pair], 1),
                        jnp.concatenate([blocks[i] for i in pair], 1),
                    )
                    total = term if total is None else total + term
        return total

    def spread_sums(r, terms, out_ref, slot, carried=None):
        for q in range(cols):
            for j in range(0, width, 2):
                pair = range(j, min(j + 2, width))
                total = None
                for value, key in terms:
                    blocks = groups(r, key)[q]
                    term = times(value, jnp.concatenate([blocks[i] for i in pair], 1))
                    total = term if total is None else total + term
                for s, i in enumerate(pair):
                    k = column(r, q, i)
                    part = total[:, s * depth : (s + 1) * depth]
                    if carried is not None:
                        part = part + carried[k, slot]
                    out_ref[k, slot] = part.astype(out_ref.dtype)

    def masked(r, p, at, j):
        value = r[BLOCKS][at, 0, j]
        return jnp.where(r[PATTERN][0, j, p] != 0, value, jnp.zeros_like(value))

    def first_body(r):
        value = times_transposed(own(r, 0), r[INV, 0][0, 0], FINE)
        r[X][...] = value
        send_all(r, value.astype(bf16))
        for j in range(width):
            r[OUT][0, j] = masked(r, 0, 0, j)

    out = kernel_call(
        first_body,
        {COL: col, PATTERN: pattern, BLOCKS: (factor_blocks, 0), **right(0), **inv(0)},
        {X: (panel, f32), SEND: (sent, bf16), OUT: shape_of("a")},
    )
    x = {0: out[X]}
    held["a"] = out[OUT]

    def mask_body(r):
        for name, pairs in bundles.items():
            for s, (m, l) in enumerate(pairs):
                for j in range(width):
                    value = masked(r, pair_number(m, l), pair_number(m, l), j)
                    if name in r:
                        r[name][s, j] = value
                    if l in merged and m == l + 1:
                        product = split_product(r[INV, m][0, 0], value)
                        r[OUT][l // 2, :, j * depth : (j + 1) * depth] = product.astype(bf16)

    outs = {n: shape_of(pairs) for n, pairs in bundles.items() if n != "a"}
    if merged:
        outs[OUT] = ((len(merged), depth, width * depth), bf16)
    found = kernel_call(
        mask_body,
        {PATTERN: pattern, BLOCKS: factor_blocks, WAIT: (out[SEND], None), **inv(*[l + 1 for l in merged])}, outs,
    )
    product = found.pop(OUT, None)
    held |= found
    for name in bundles:
        add_bundle(name)

    products = {0: product}
    if merged:
        for d in [1 << s for s in reversed(range((rows - 1).bit_length()))]:
            products |= {s ^ d: lax.ppermute(v, "row", [(r, r ^ d) for r in range(rows)]) for s, v in products.items()}

    gathered = {0: (swap(out[SEND]), ANYWHERE)}
    y, rounded = {}, {}

    def panels(lower):
        return {(PANEL, l): gathered[l] for l in lower}

    for m in range(1, levels):
        def solve_body(r):
            value = times_transposed(own(r, m) - sum_over(r, m, range(m)), r[INV, m][0, 0], FINE)
            if m < top:
                r[X][...] = value
                send_all(r, value.astype(bf16))
                return
            for l in range(top):
                r[STACK][l] = r[X, l][...]
            r[STACK][top] = value
            result = times(value, r[INV, m][0, 0], FINE)
            r[Y][...] = result
            r[V][...] = result.astype(bf16)
            spread_sums(r, [(result.astype(bf16), (m, m - 1))], r[SEND], 0)

        outs = {X: (panel, f32), SEND: (sent, bf16)}
        if m == top:
            outs = {STACK: ((levels,) + panel, f32), Y: (panel, f32), V: (panel, bf16)}
            outs |= {SEND: ((rows, 1, chunk, depth), bf16)}
        out = kernel_call(
            solve_body,
            {COL: col, **right(m), **inv(m), **panels(range(m)), **need(*[(m, l) for l in range(m)])}
            | {(X, l): x[l] for l in range(top) if m == top}, outs,
        )
        if m < top:
            x[m] = out[X]
            gathered[m] = (swap(out[SEND]), ANYWHERE)
    y[top], rounded[top] = out[Y], out[V]
    solved = out[STACK]

    wanted = [(m, l) for l in reversed(merged) for m in range(l + 2, levels)]
    if merged:
        first = [key for key in wanted if key[1] == merged[-1]]
        fixed = {"d": first, "g": wanted[len(first) :]}

        def fix_body(r):
            for s in range(rows):
                r[ALL][r[ROW][0] ^ s] = r[FAR, s][...]
            for n, s, m, l in [(n, s, *key) for n, keys in fixed.items() for s, key in enumerate(keys)]:
                total = None
                for q, blocks in enumerate(groups(r, (m, l + 1))):
                    for j in range(0, width, 2):
                        pair = range(j, min(j + 2, width))
                        term = times(
                            jnp.concatenate([blocks[i] for i in pair], 1),
                            jnp.concatenate([r[ALL][column(r, q, i), l // 2] for i in pair], 0),
                        )
                        total = term if total is None else total + term
                for j in range(width):
                    raw = groups(r, (m, l))[0][j].astype(f32)
                    r[n][s, j] = (raw - total[:, j * depth : (j + 1) * depth]).astype(bf16)

        held |= kernel_call(
            fix_body,
            {COL: col, ROW: row, **{(FAR, s): (v, ANYWHERE) for s, v in products.items()}}
            | need(*wanted, *[(m, l + 1) for m, l in wanted]),
            {n: shape_of(keys) for n, keys in fixed.items()}, {ALL: ((rows,) + product.shape, bf16)},
        )
        for n, keys in fixed.items():
            add_bundle(n)
            for s, (m, l) in enumerate(keys):
                place[m, l, True] = (n, s)

    lower = [(l, l + 1) for l in reversed(merged)] if merged else [(l,) for l in range(top - 2, -1, -1)]
    plan = [(top - 1,)] + lower

    def terms_for(l, values):
        return [(v, (m, l, True) if (m, l) in wanted else (m, l)) for m, v in values.items()]

    def pairs_for(targets, upper):
        return need(*[key for l in targets for _, key in terms_for(l, dict.fromkeys(upper))])

    for s, done in enumerate(plan):
        targets = plan[s + 1] if s + 1 < len(plan) else ()
        upper = range(done[-1] + 1, levels)
        stacks = s + 2 == len(plan)
        arrived = (swap(out[SEND]), ANYWHERE)
        slots = (rows, max(len(targets), 1), chunk, depth)
        ins = {COL: col, ARRIVED: arrived, **inv(*done), **{(X, m): x[m] for m in done}}
        if targets:
            odds = [l + 1 for l in targets if l in merged]

            def carry_terms(r):
                values = {m: r[V, m][...] for m in upper}
                terms = {l: terms_for(l, values) for l in targets}
                for m in odds:
                    own_part = times(r[X, m][...], r[INV, m][0, 0], FINE).astype(bf16)
                    terms[m - 1].append((own_part, (m, m - 1)))
                return terms

            known = {(V, m): rounded[m] for m in upper} | {(X, m): x[m] for m in odds} | inv(*odds)
            known |= pairs_for(targets, upper) | need(*[(m, m - 1) for m in odds])
            if s > 0:
                def carry_body(r):
                    for slot, (l, terms) in enumerate(carry_terms(r).items()):
                        spread_sums(r, terms, r[CARRY], slot)

                known = kernel_call(carry_body, {COL: col, **known}, {CARRY: (slots, f32)})
            ins |= {**known, **pairs_for(targets, done)}

        def step_body(r):
            values = {}
            for slot, m in enumerate(done):
                total = r[ARRIVED][0, slot].astype(f32)
                for k in range(1, rows):
                    total = total + r[ARRIVED][k, slot].astype(f32)
                result = times(r[X, m][...] - total, r[INV, m][0, 0], FINE)
                if not targets:
                    r[OUT][slot] = result
                    continue
                if stacks:
                    r[STACK][m - len(targets)] = result
                else:
                    r[Y, m][...] = result
                values[m] = result.astype(bf16)
                r[V, m][...] = values[m]
            for m in upper if stacks else ():
                r[STACK][m - len(targets)] = r[Y, m][...]
            folded = carry_terms(r) if targets and s == 0 else {}
            for slot, l in enumerate(targets):
                spread_sums(r, terms_for(l, values) + folded.get(l, []), r[SEND], slot, r.get(CARRY))

        if targets:
            outs = {(V, m): (panel, bf16) for m in done} | {SEND: (slots, bf16)}
            if stacks:
                outs[STACK] = ((levels - len(targets),) + panel, f32)
                ins |= {(Y, m): y[m] for m in upper}
            else:
                outs |= {(Y, m): (panel, f32) for m in done}
        else:
            outs = {OUT: ((len(done),) + panel, f32)}
        out = kernel_call(step_body, ins, outs)
        if targets:
            for m in done:
                y[m], rounded[m] = out.get((Y, m)), out[V, m]
            high = out.get(STACK)

    def pieces(value):
        found = {q: exchange(value, q, cols) for q in range(cols - 1, 0, -1)}
        return [value] + [found[q] for q in range(1, cols)]

    def joined(*runs):
        def join_body(r):
            at = 0
            for s, run in enumerate(runs):
                count = run[0].shape[0]
                for q in range(cols):
                    where = pl.ds(pl.multiple_of((r[COL][0] ^ q) * chunk, chunk), chunk)
                    r[OUT][pl.ds(at, count), where, :] = r[X, s, q][...]
                at += count

        ins = {(X, s, q): (v, ANYWHERE if q else -1) for s, run in enumerate(runs) for q, v in enumerate(run)}
        return kernel_call(join_body, {COL: col, **ins}, {OUT: ((levels, rhs, depth), f32)})[OUT][:, None]

    last = pieces(out[OUT])
    forward = joined(pieces(solved))
    return forward, joined(last, pieces(high))


def solution(mesh):
    rows, cols = mesh.shape["row"], mesh.shape["col"]
    placed = (
        P(None, "row", None, None),
        P(None, "row", None, None),
        P(None, "row", "col", None, None),
        P(None, "row", "col"),
    )
    return jax.shard_map(
        functools.partial(shards, rows, cols),
        mesh=mesh,
        in_specs=placed,
        out_specs=(P(None, "row", None, None), P(None, "row", None, None)),
        check_vma=False,
    )
```

```python
import functools
import math
import jax
import jax.numpy as jnp
from jax import lax
from jax.experimental import pallas as pl
from jax.experimental.pallas import tpu as pltpu
from jax.sharding import PartitionSpec as P

MERGE_BYTES = 24 << 20
f32, bf16 = jnp.float32, jnp.bfloat16
ANYWHERE = -2


def pair_number(higher, lower_level):
    return higher * (higher - 1) // 2 + lower_level


def times_transposed(v, g):
    return lax.dot_general(v, g, (((1,), (1,)), ((), ())), preferred_element_type=f32)


def times(v, g):
    return lax.dot_general(v, g, (((1,), (0,)), ((), ())), preferred_element_type=f32)


def halves(d):
    high = d.astype(bf16)
    return high, (d - high.astype(f32)).astype(bf16)


def fine(product, v, d):
    (v_high, v_low), (d_high, d_low) = halves(v), halves(d)
    rows = v.shape[0]
    both = jnp.concatenate([v_high, v_low], 0)
    large, small = product(both, d_high), product(both, d_low)
    return large[:rows] + (large[rows:] + (small[:rows] + small[rows:]))


def split_product(d, g):
    high, low = halves(d)
    return times(high, g) + times(low, g)


def kernel_call(body, ins, outs, scratch=None):
    in_keys, out_keys, scratch = list(ins), list(outs), scratch or {}
    arrays, specs, held = [], [], 0
    for value in ins.values():
        array, at = value if isinstance(value, tuple) else (value, -1)
        if array.dtype == jnp.int32:
            if array.size > 1:
                array = pltpu.with_memory_space_constraint(array, pltpu.HBM)
            specs.append(pl.BlockSpec(memory_space=pltpu.SMEM))
        elif at is None:
            array = pltpu.with_memory_space_constraint(array, pltpu.HBM)
            specs.append(pl.BlockSpec(memory_space=pltpu.HBM))
        else:
            shape = array.shape
            if at >= 0:
                shape = (1,) + shape[1:]
            if at > -2:
                array = pltpu.with_memory_space_constraint(array, pltpu.HBM)
            index = (max(at, 0),) + (0,) * (len(shape) - 1)
            specs.append(pl.BlockSpec(shape, lambda *_, index=index: index))
            held += math.prod(shape) * array.dtype.itemsize
        arrays.append(array)
    shapes = list(outs.values())
    if len(shapes) == 1:
        shapes.append(((8, 128), f32))
    held += sum(math.prod(s[0]) * jnp.dtype(s[1]).itemsize for s in shapes)

    def kernel(*refs):
        spare = [None] * (len(shapes) - len(out_keys))
        body(dict(zip(in_keys + out_keys + spare + list(scratch), refs)))
        if spare:
            last = refs[len(in_keys) + 1]
            last[...] = jnp.zeros(last.shape, f32)

    values = pl.pallas_call(
        kernel,
        grid=(1,),
        out_shape=[(pltpu.VMEM if len(s) > 2 else pltpu.HBM)(s[0], s[1]) for s in shapes],
        in_specs=specs,
        out_specs=[pl.BlockSpec(s[0], lambda *_, d=len(s[0]): (0,) * d) for s in shapes],
        scratch_shapes=[pltpu.VMEM(*s) for s in scratch.values()],
        compiler_params=pltpu.CompilerParams(vmem_limit_bytes=2 * held + (4 << 20)),
    )(*arrays)
    return dict(zip(out_keys, values))


def exchange(value, step, size):
    return lax.ppermute(value, "col", [(c, c ^ step) for c in range(size)])


def shards(rows, cols, right_side, inverses, factor_blocks, pattern):
    return body_of(rows, cols, right_side, inverses, factor_blocks, pattern)


def body_of(rows, cols, right_side, inverses, factor_blocks, pattern):
    levels, _, rhs, depth = right_side.shape
    width = factor_blocks.shape[2]
    chunk = rhs // cols
    top = levels - 1
    pattern = jnp.transpose(pattern, (1, 2, 0))
    col = lax.axis_index("col").reshape(1).astype(jnp.int32)
    row = lax.axis_index("row").reshape(1).astype(jnp.int32)
    panel, sent = (chunk, depth), (rows, chunk, depth)
    block = depth * depth * factor_blocks.dtype.itemsize
    sizes = factor_blocks.shape[0] * cols * width * block + 6 * rows * width * block
    merging = sizes <= MERGE_BYTES and levels % 2 == 0 and rows & (rows - 1) == 0
    merged = range(0, top - 1, 2) if merging else ()
    steps = [1 << s for s in reversed(range((cols - 1).bit_length()))]

    COL, ROW, PATTERN, BLOCKS, WAIT, ARRIVED, CARRY, SEND, OUT, ALL, STACK = range(11)
    INV, RIGHT, PANEL, X, Y, V, FAR = range(11, 18)

    def inv(*ms):
        return {(INV, m): (inverses, m) for m in ms}

    def right(m):
        return {(RIGHT, m): (right_side, m)}

    def own(r, m):
        return r[RIGHT, m][0, 0, pl.ds(pl.multiple_of(r[COL][0] * chunk, chunk), chunk), :]

    def swap(value):
        return lax.all_to_all(value, "row", 0, 0)

    def send_all(r, value):
        for k in range(rows):
            r[SEND][k] = value

    cuts = [(1, 2), (2, 4), (4, levels)]
    bundles = {n: [(m, l) for m in range(*cut) for l in range(m)] for n, cut in zip("abc", cuts)}
    place = {pair: (n, s) for n, pairs in bundles.items() for s, pair in enumerate(pairs)}
    held, arrays = {}, {}

    def near(name, q):
        return merging and q > 0 and name in "bcd"

    def shape_of(pairs):
        return (len(pairs), width, depth, depth), bf16

    def add_bundle(name):
        found = {0: held[name]}
        if name == "a":
            found |= {q: exchange(held[name], q, cols) for q in range(cols - 1, 0, -1)}
        for step in steps if name != "a" else ():
            found |= {q ^ step: exchange(v, step, cols) for q, v in found.items()}
        for q, v in found.items():
            arrays[name, q] = pltpu.with_memory_space_constraint(v, pltpu.VMEM) if near(name, q) else v

    def need(*keys):
        found = {}
        for n, s in sorted({place[k] for k in keys}):
            for q in range(cols):
                v = arrays[n, q]
                if near(n, q):
                    found[n, q] = (v, ANYWHERE)
                else:
                    found[n, s, q] = (v, ANYWHERE if v.shape[0] == 1 else s)
        return found

    def groups(r, key):
        name, s = place[key]
        return [r[name, q].at[s] if near(name, q) else r[name, s, q].at[0] for q in range(cols)]

    def column(r, q, j):
        return (r[COL][0] ^ q) * width + j

    def sum_over(r, m, lower):
        total = None
        for l in lower:
            for q, blocks in enumerate(groups(r, (m, l))):
                for j in range(0, width, 2):
                    pair = range(j, min(j + 2, width))
                    term = times_transposed(
                        jnp.concatenate([r[PANEL, l][column(r, q, i)] for i in pair], 1),
                        jnp.concatenate([blocks[i] for i in pair], 1),
                    )
                    total = term if total is None else total + term
        return total

    def spread_sums(r, terms, out_ref, slot, carried=None):
        for q in range(cols):
            for j in range(0, width, 2):
                pair = range(j, min(j + 2, width))
                total = None
                for value, key in terms:
                    blocks = groups(r, key)[q]
                    term = times(value, jnp.concatenate([blocks[i] for i in pair], 1))
                    total = term if total is None else total + term
                for s, i in enumerate(pair):
                    k = column(r, q, i)
                    part = total[:, s * depth : (s + 1) * depth]
                    if carried is not None:
                        part = part + carried[k, slot]
                    out_ref[k, slot] = part.astype(out_ref.dtype)

    def masked(r, p, at, j):
        value = r[BLOCKS][at, 0, j]
        return jnp.where(r[PATTERN][0, j, p] != 0, value, jnp.zeros_like(value))

    def first_body(r):
        value = fine(times_transposed, own(r, 0), r[INV, 0][0, 0])
        r[X][...] = value
        send_all(r, value.astype(bf16))
        for j in range(width):
            r[OUT][0, j] = masked(r, 0, 0, j)

    out = kernel_call(
        first_body,
        {COL: col, PATTERN: pattern, BLOCKS: (factor_blocks, 0), **right(0), **inv(0)},
        {X: (panel, f32), SEND: (sent, bf16), OUT: shape_of("a")},
    )
    x = {0: out[X]}
    held["a"] = out[OUT]

    def mask_body(r):
        for name, pairs in bundles.items():
            for s, (m, l) in enumerate(pairs):
                for j in range(width):
                    value = masked(r, pair_number(m, l), pair_number(m, l), j)
                    if name in r:
                        r[name][s, j] = value
                    if l in merged and m == l + 1:
                        product = split_product(r[INV, m][0, 0], value)
                        r[OUT][l // 2, :, j * depth : (j + 1) * depth] = product.astype(bf16)

    outs = {n: shape_of(pairs) for n, pairs in bundles.items() if n != "a"}
    if merged:
        outs[OUT] = ((len(merged), depth, width * depth), bf16)
    found = kernel_call(
        mask_body,
        {PATTERN: pattern, BLOCKS: factor_blocks, WAIT: (out[SEND], None), **inv(*[l + 1 for l in merged])}, outs,
    )
    product = found.pop(OUT, None)
    held |= found
    for name in bundles:
        add_bundle(name)

    products = {0: product}
    if merged:
        for d in [1 << s for s in reversed(range((rows - 1).bit_length()))]:
            products |= {s ^ d: lax.ppermute(v, "row", [(r, r ^ d) for r in range(rows)]) for s, v in products.items()}

    gathered = {0: (swap(out[SEND]), ANYWHERE)}
    y, rounded = {}, {}

    def panels(lower):
        return {(PANEL, l): gathered[l] for l in lower}

    for m in range(1, levels):
        def solve_body(r):
            value = fine(times_transposed, own(r, m) - sum_over(r, m, range(m)), r[INV, m][0, 0])
            if m < top:
                r[X][...] = value
                send_all(r, value.astype(bf16))
                return
            for l in range(top):
                r[STACK][l] = r[X, l][...]
            r[STACK][top] = value
            result = fine(times, value, r[INV, m][0, 0])
            r[Y][...] = result
            r[V][...] = result.astype(bf16)
            spread_sums(r, [(result.astype(bf16), (m, m - 1))], r[SEND], 0)

        outs = {X: (panel, f32), SEND: (sent, bf16)}
        if m == top:
            outs = {STACK: ((levels,) + panel, f32), Y: (panel, f32), V: (panel, bf16)}
            outs |= {SEND: ((rows, 1, chunk, depth), bf16)}
        out = kernel_call(
            solve_body,
            {COL: col, **right(m), **inv(m), **panels(range(m)), **need(*[(m, l) for l in range(m)])}
            | {(X, l): x[l] for l in range(top) if m == top}, outs,
        )
        if m < top:
            x[m] = out[X]
            gathered[m] = (swap(out[SEND]), ANYWHERE)
    y[top], rounded[top] = out[Y], out[V]
    solved = out[STACK]

    wanted = [(m, l) for l in reversed(merged) for m in range(l + 2, levels)]
    if merged:
        first = [key for key in wanted if key[1] == merged[-1]]
        fixed = {"d": first, "g": wanted[len(first) :]}

        def fix_body(r):
            for s in range(rows):
                r[ALL][r[ROW][0] ^ s] = r[FAR, s][...]
            for n, s, m, l in [(n, s, *key) for n, keys in fixed.items() for s, key in enumerate(keys)]:
                total = None
                for q, blocks in enumerate(groups(r, (m, l + 1))):
                    for j in range(0, width, 2):
                        pair = range(j, min(j + 2, width))
                        term = times(
                            jnp.concatenate([blocks[i] for i in pair], 1),
                            jnp.concatenate([r[ALL][column(r, q, i), l // 2] for i in pair], 0),
                        )
                        total = term if total is None else total + term
                for j in range(width):
                    raw = groups(r, (m, l))[0][j].astype(f32)
                    r[n][s, j] = (raw - total[:, j * depth : (j + 1) * depth]).astype(bf16)

        held |= kernel_call(
            fix_body,
            {COL: col, ROW: row, **{(FAR, s): (v, ANYWHERE) for s, v in products.items()}}
            | need(*wanted, *[(m, l + 1) for m, l in wanted]),
            {n: shape_of(keys) for n, keys in fixed.items()}, {ALL: ((rows,) + product.shape, bf16)},
        )
        for n, keys in fixed.items():
            add_bundle(n)
            for s, (m, l) in enumerate(keys):
                place[m, l, True] = (n, s)

    lower = [(l, l + 1) for l in reversed(merged)] if merged else [(l,) for l in range(top - 2, -1, -1)]
    plan = [(top - 1,)] + lower

    def terms_for(l, values):
        return [(v, (m, l, True) if (m, l) in wanted else (m, l)) for m, v in values.items()]

    def pairs_for(targets, upper):
        return need(*[key for l in targets for _, key in terms_for(l, dict.fromkeys(upper))])

    for s, done in enumerate(plan):
        targets = plan[s + 1] if s + 1 < len(plan) else ()
        upper = range(done[-1] + 1, levels)
        stacks = s + 2 == len(plan)
        arrived = (swap(out[SEND]), ANYWHERE)
        slots = (rows, max(len(targets), 1), chunk, depth)
        ins = {COL: col, ARRIVED: arrived, **inv(*done), **{(X, m): x[m] for m in done}}
        if targets:
            odds = [l + 1 for l in targets if l in merged]

            def carry_terms(r):
                values = {m: r[V, m][...] for m in upper}
                terms = {l: terms_for(l, values) for l in targets}
                for m in odds:
                    own_part = fine(times, r[X, m][...], r[INV, m][0, 0]).astype(bf16)
                    terms[m - 1].append((own_part, (m, m - 1)))
                return terms

            known = {(V, m): rounded[m] for m in upper} | {(X, m): x[m] for m in odds} | inv(*odds)
            known |= pairs_for(targets, upper) | need(*[(m, m - 1) for m in odds])
            if s > 0:
                def carry_body(r):
                    for slot, (l, terms) in enumerate(carry_terms(r).items()):
                        spread_sums(r, terms, r[CARRY], slot)

                known = kernel_call(carry_body, {COL: col, **known}, {CARRY: (slots, f32)})
            ins |= {**known, **pairs_for(targets, done)}

        def step_body(r):
            values = {}
            for slot, m in enumerate(done):
                total = r[ARRIVED][0, slot].astype(f32)
                for k in range(1, rows):
                    total = total + r[ARRIVED][k, slot].astype(f32)
                result = fine(times, r[X, m][...] - total, r[INV, m][0, 0])
                if not targets:
                    r[OUT][slot] = result
                    continue
                if stacks:
                    r[STACK][m - len(targets)] = result
                else:
                    r[Y, m][...] = result
                values[m] = result.astype(bf16)
                r[V, m][...] = values[m]
            for m in upper if stacks else ():
                r[STACK][m - len(targets)] = r[Y, m][...]
            folded = carry_terms(r) if targets and s == 0 else {}
            for slot, l in enumerate(targets):
                spread_sums(r, terms_for(l, values) + folded.get(l, []), r[SEND], slot, r.get(CARRY))

        if targets:
            outs = {(V, m): (panel, bf16) for m in done} | {SEND: (slots, bf16)}
            if stacks:
                outs[STACK] = ((levels - len(targets),) + panel, f32)
                ins |= {(Y, m): y[m] for m in upper}
            else:
                outs |= {(Y, m): (panel, f32) for m in done}
        else:
            outs = {OUT: ((len(done),) + panel, f32)}
        out = kernel_call(step_body, ins, outs)
        if targets:
            for m in done:
                y[m], rounded[m] = out.get((Y, m)), out[V, m]
            high = out.get(STACK)

    def pieces(value):
        found = {q: exchange(value, q, cols) for q in range(cols - 1, 0, -1)}
        return [value] + [found[q] for q in range(1, cols)]

    def joined(*runs):
        def join_body(r):
            at = 0
            for s, run in enumerate(runs):
                count = run[0].shape[0]
                for q in range(cols):
                    where = pl.ds(pl.multiple_of((r[COL][0] ^ q) * chunk, chunk), chunk)
                    r[OUT][pl.ds(at, count), where, :] = r[X, s, q][...]
                at += count

        ins = {(X, s, q): (v, ANYWHERE if q else -1) for s, run in enumerate(runs) for q, v in enumerate(run)}
        return kernel_call(join_body, {COL: col, **ins}, {OUT: ((levels, rhs, depth), f32)})[OUT][:, None]

    last = pieces(out[OUT])
    forward = joined(pieces(solved))
    return forward, joined(last, pieces(high))


def solution(mesh):
    rows, cols = mesh.shape["row"], mesh.shape["col"]
    placed = (
        P(None, "row", None, None),
        P(None, "row", None, None),
        P(None, "row", "col", None, None),
        P(None, "row", "col"),
    )
    return jax.shard_map(
        functools.partial(shards, rows, cols),
        mesh=mesh,
        in_specs=placed,
        out_specs=(P(None, "row", None, None), P(None, "row", None, None)),
        check_vma=False,
    )
```
